128 devices in a mesh: row: 8 (over z, core), col: 16 (over x, y).
Axes of the slice: x: 4, y: 4, z: 4, core: 2. Of those that a mesh axis runs over, the one named last changes fastest.
Arguments:
- covariance: float32 [9216, 9216], P('row', 'col'), as said below
- features: float32 [2, 9216, 128], P(None, ('row', 'col')), may hold values from -6 to 6
- noise: float32 [2, 128], replicated, may hold values from 2304 to 36864
Outputs:
- updated: float32 [9216, 9216], P('row', 'col')
The draws below stay inside these ranges and needn't reach their ends.
Inputs may be any that keep to these rules, and one draw needn't show every extreme that they name: covariance is symmetric and positive definite.
All inputs are finite; a program needn't handle non-finite values.
Results may differ from the reference program's by a relative error of at most 0.0001.
Values sent between devices are 32-bit elements; how exact they have to be, the bound alone decides.
No kernel may reach another device: no remote copies, remote signals or barrier semaphores. Data moves between devices by JAX's collectives and lax.ppermute only.
A program may use at most 64 MiB of HBM per device.

```python
import math
import jax
import jax.numpy as jnp
from jax import lax

FF = 9216
BATCH = 128
STEPS = 2


def draw_covariance(key, part):
    first, second = jax.random.split(jax.random.fold_in(key, 7))
    base = jax.random.normal(first, (FF, FF), jnp.float32)
    offdiag = (base + base.T) * (0.3 / jnp.sqrt(2.0 * FF))
    scales = jnp.exp(jax.random.uniform(second, (FF,), jnp.float32, 0.0, 0.6931472))
    return offdiag + jnp.diag(scales)


def block_levels(rng, dims, shards, low, top_value):
    def one(axis_at, blocks):
        heights = jax.random.uniform(jax.random.fold_in(jax.random.fold_in(rng, 6), axis_at), (blocks,), jnp.float32, low / len(shards), top_value / len(shards))
        return jnp.repeat(jnp.exp(heights), dims[axis_at] // blocks).reshape((-1,) + (1,) * (len(dims) - axis_at - 1))

    level = one(*shards[0])
    for cut in shards[1:]:
        level = level * one(*cut)
    return level


def normal_values(stream_key, dims, width, reach, cuts=(), held_as=jnp.bfloat16):
    array = width * jax.random.normal(stream_key, dims, jnp.float32)
    if cuts:
        array = array * block_levels(stream_key, dims, cuts, -0.22, 0.18)
    return jnp.clip(array, -reach, reach).astype(held_as)


def setup_inputs(seed: int = 0) -> dict:
    seeds = jax.random.split(jax.random.key(seed), 4)
    return {
        "covariance": draw_covariance(jax.random.fold_in(seeds[3], 71), 0),
        "features": normal_values(seeds[1], (STEPS, FF, BATCH), 1.0, 6.0, ((1, 128),), jnp.float32),
        "noise": jnp.clip(jnp.exp(jax.random.uniform(seeds[2], (STEPS, BATCH), jnp.float32, math.log(2304.0), math.log(36864.0))), 2304.0, 36864.0),
    }


def invert(system):
    lower = jnp.linalg.cholesky(system)
    eye = jnp.eye(system.shape[0], dtype=system.dtype)
    middle = lax.linalg.triangular_solve(lower, eye, left_side=True, lower=True)
    return lax.linalg.triangular_solve(lower, middle, left_side=True, lower=True, transpose_a=True)

def reference(covariance, features, noise):
    highest = lax.Precision.HIGHEST
    matrix = covariance
    for step in range(STEPS):
        block = features[step]
        product = jnp.dot(matrix.astype(jnp.float32), block.astype(jnp.float32), precision=highest, preferred_element_type=jnp.float32)
        system = jnp.dot(block.T.astype(jnp.float32), product.astype(jnp.float32), precision=highest, preferred_element_type=jnp.float32) + jnp.diag(noise[step])
        inverse = invert(system)
        gain = jnp.dot(product.astype(jnp.float32), inverse.astype(jnp.float32), precision=highest, preferred_element_type=jnp.float32)
        matrix = matrix - jnp.dot(gain.astype(jnp.float32), product.T.astype(jnp.float32), precision=highest, preferred_element_type=jnp.float32)
    return matrix
```

```python
import jax
import jax.numpy as jnp
from jax import lax
from jax.experimental import pallas as pl
from jax.experimental.pallas import tpu as pltpu
from jax.sharding import PartitionSpec as P

HIGHEST = lax.Precision.HIGHEST
HIGH = lax.Precision.HIGH


def dot(a, b, dims, precision):
    return lax.dot_general(a, b, (dims, ((), ())), precision=precision, preferred_element_type=jnp.float32)


def to_xor(value, axis, bits):
    size = lax.axis_size(axis)
    return lax.ppermute(value, axis, [(i, i ^ bits) for i in range(size)])


def from_ring(value, axis, unit):
    return [to_xor(value, axis, unit * d) for d in (1, 2, 3)]


def placed(pieces, places, count):
    height = pieces[0].shape[0]
    out = jnp.zeros((count * height, *pieces[0].shape[1:]), pieces[0].dtype)
    for piece, place in zip(pieces, places):
        out = lax.dynamic_update_slice_in_dim(out, piece, place * height, 0)
    return out


def column_owner(index):
    col, part = index // 8, index % 8
    return part * 16 + col


def row_owner(index):
    r, c = index // 16, index % 16
    zs, cs, x, y = r // 2, r % 2, c // 4, c % 4
    core = y // 2
    yt = y if cs == core else y ^ 3
    return (2 * x + core) * 16 + 4 * zs + yt


def invert_kernel(m_ref, noise_ref, out_ref):
    n = m_ref.shape[0]
    eye = lax.broadcasted_iota(jnp.int32, (n, n), 0) == lax.broadcasted_iota(jnp.int32, (n, n), 1)
    one = jnp.where(eye, 1.0, 0.0).astype(jnp.float32)
    system = m_ref[...] + jnp.where(eye, noise_ref[...], 0.0)
    diag = jnp.where(eye, system, 0.0)
    across = lax.rsqrt(jnp.sum(diag, axis=0, keepdims=True))
    down = lax.rsqrt(jnp.sum(diag, axis=1, keepdims=True))
    scaled = system * down * across
    bound = jnp.max(jnp.sum(jnp.abs(scaled), axis=1, keepdims=True), axis=0, keepdims=True)
    alpha = 2.0 / (1.0 + bound)
    err = one - alpha * scaled
    start = alpha * (one + err)

    def fast(a, b):
        return jnp.dot(a.astype(jnp.bfloat16), b.astype(jnp.bfloat16), preferred_element_type=jnp.float32)

    def full(a, b):
        return jnp.dot(a, b, precision=HIGHEST, preferred_element_type=jnp.float32)

    err2 = fast(err, err)
    err4 = fast(err2, err2)
    guess = start + fast(start, err2)
    guess = guess + fast(guess, err4)

    def norm(r):
        return jnp.max(jnp.sum(jnp.abs(r), axis=0, keepdims=True))

    rest = one - full(scaled, guess)
    size = norm(rest)
    bad = size >= 0.5
    guess = jnp.where(bad, start, guess)

    def go_on(state):
        return jnp.logical_and(state[1] >= 1e-3, state[2] < 60)

    def refine(state):
        y = state[0]
        r = one - full(scaled, y)
        return y + full(y, r), norm(r), state[2] + 1

    guess, _, _ = lax.while_loop(go_on, refine, (guess, jnp.float32(1.0), jnp.int32(0)))
    out_ref[...] = guess * down * across


def inverse_of(m, noise):
    n = m.shape[0]
    return pl.pallas_call(
        invert_kernel,
        out_shape=jax.ShapeDtypeStruct((n, n), jnp.float32),
        cost_estimate=pl.CostEstimate(flops=2 * n**3 * 40, bytes_accessed=4 * n * n * 3, transcendentals=n),
    )(m, noise)


def body(covariance, features, noise):
    r, c = lax.axis_index("row"), lax.axis_index("col")
    z, core, x, y = r // 2, r % 2, c // 4, c % 4
    steps, block, batch = features.shape
    width = steps * batch
    own = jnp.moveaxis(features, 0, 1).reshape(block, width)

    apart = lax.ppermute(own, ("row", "col"), [(i, column_owner(i)) for i in range(128)])
    line = placed([own, *from_ring(own, "col", 1)], [y ^ d for d in range(4)], 4)
    plane = [line, *from_ring(line, "col", 4)]
    pair = placed([apart, to_xor(apart, "row", 1)], [core, core ^ 1], 2)
    column_features = placed([pair, *from_ring(pair, "row", 2)], [z ^ d for d in range(4)], 4)
    row_features = placed(plane, [x ^ d for d in range(4)], 4)

    partial = dot(covariance, row_features, ((0,), (0,)), HIGH)
    inner = dot(column_features, partial, ((0,), (0,)), HIGHEST)
    m_rows = width // 8
    both = jnp.concatenate(
        [partial.reshape(4, 2, block, width), inner.reshape(4, 2, m_rows, width)], axis=2
    )
    kept = lax.dynamic_index_in_dim(both, core, 1, keepdims=False)
    given = lax.dynamic_index_in_dim(both, core ^ 1, 1, keepdims=False)
    chip = kept + to_xor(given, "row", 1)
    total = lax.dynamic_index_in_dim(chip, z, 0, keepdims=False)
    arrived = [
        to_xor(lax.dynamic_index_in_dim(chip, z ^ d, 0, keepdims=False), "row", 2 * d) for d in (1, 2, 3)
    ]
    total = total + arrived[0] + arrived[1] + arrived[2]
    product, share = total[:block], total[block:]

    for unit in (1, 4):
        a1, a2, a3 = from_ring(share, "col", unit)
        share = (share + a1) + (a2 + a3)
    share_pair = placed([share, to_xor(share, "row", 1)], [core, core ^ 1], 2)
    matrix = placed([share_pair, *from_ring(share_pair, "row", 2)], [z ^ d for d in range(4)], 4)

    moved = lax.ppermute(product, ("row", "col"), [(i, row_owner(i)) for i in range(128)])
    pieces = [moved, *from_ring(moved, "col", 1)]
    slots = []
    for d in range(4):
        w = d ^ y ^ (2 * core)
        far = w // 2
        b = jnp.where(far == 1, w ^ 3, w)
        slots.append(2 * b + (far ^ core))
    product_line = placed(pieces, slots, 4).reshape(2, 1, 2 * block, width)
    out = jnp.zeros((2, 4, 2 * block, width), jnp.float32)
    lines = [product_line, *from_ring(product_line, "col", 4)]
    for d, piece in enumerate(lines):
        out = lax.dynamic_update_slice_in_dim(out, piece, x ^ d, 1)
    product_rows = out.reshape(16 * block, width)
    product_pair = placed([product, to_xor(product, "row", 1)], [core, core ^ 1], 2)
    product_cols = placed([product_pair, *from_ring(product_pair, "row", 2)], [z ^ d for d in range(4)], 4)

    inverse = inverse_of(matrix, noise.reshape(1, width))
    gain = dot(product_rows, inverse, ((1,), (0,)), HIGH)
    return covariance - dot(gain, product_cols, ((1,), (1,)), HIGH)


def solution(mesh):
    specs = (P("row", "col"), P(None, ("row", "col"), None), P())
    return jax.shard_map(body, mesh=mesh, in_specs=specs, out_specs=P("row", "col"), check_vma=False)
```

```python
import jax
import jax.numpy as jnp
from jax import lax
from jax.experimental import pallas as pl
from jax.experimental.pallas import tpu as pltpu
from jax.sharding import PartitionSpec as P


HIGHEST = lax.Precision.HIGHEST
HIGH = lax.Precision.HIGH


def dot(a, b, dims, precision):
    return lax.dot_general(a, b, (dims, ((), ())), precision=precision, preferred_element_type=jnp.float32)


def to_xor(value, axis, bits):
    size = lax.axis_size(axis)
    return lax.ppermute(value, axis, [(i, i ^ bits) for i in range(size)])


def to_place(value, owner):
    return lax.ppermute(value, ("row", "col"), [(i, owner(i)) for i in range(128)])


def side(a, b, bit):
    first = jnp.where(bit == 0, a, b)
    second = jnp.where(bit == 0, b, a)
    return jnp.stack([first, second])


def feature_place(index):
    col, part = index // 8, index % 8
    return (2 * (part % 4) + part // 4) * 16 + col


def product_place(index):
    row, col = index // 16, index % 16
    return 8 * col + 4 * (row % 2) + row // 2


def to_plane(block):
    devices = lax.axis_size("col")
    sent = jnp.broadcast_to(block[None], (devices, *block.shape))
    return lax.all_to_all(sent, "col", 0, 0, tiled=True).reshape(-1, block.shape[-1])


def halves(a):
    high = a.astype(jnp.bfloat16)
    return high, (a - high.astype(jnp.float32)).astype(jnp.bfloat16)


def near_full(a, b, dims):
    (ah, al), (bh, bl) = a, b
    dims = (dims, ((), ()))

    def one(p, q):
        return lax.dot_general(p, q, dims, preferred_element_type=jnp.float32)

    return one(ah, bh) + (one(ah, bl) + one(al, bh))


def products_kernel(core_ref, cov_ref, rows_ref, cols_ref, kept_ref, given_ref, t_ref, m_ref):
    core = core_ref[0]
    block, share = t_ref.shape[0] // 8, m_ref.shape[0] // 8
    part = near_full(halves(cov_ref[...]), halves(rows_ref[...]), ((1,), (0,)))
    t_ref[...] = part
    m_ref[...] = near_full(halves(cols_ref[...]), halves(part), ((0,), (0,)))
    for ref, at in ((kept_ref, core), (given_ref, 1 - core)):
        for i in range(4):
            ref[i, :block, :] = t_ref[pl.ds(pl.multiple_of((4 * at + i) * block, 8), block), :]
            ref[i, block:, :] = m_ref[pl.ds(pl.multiple_of((4 * at + i) * share, 8), share), :]


def products(core, cov, rows, cols):
    n, width = cols.shape
    depth = n // 8 + width // 8
    exchange = jax.ShapeDtypeStruct((4, depth, width), jnp.float32)
    return pl.pallas_call(
        products_kernel,
        out_shape=(exchange, exchange),
        in_specs=[pl.BlockSpec(memory_space=pltpu.SMEM)] + [pl.BlockSpec(memory_space=pltpu.VMEM)] * 3,
        scratch_shapes=[pltpu.VMEM((n, width), jnp.float32), pltpu.VMEM((width, width), jnp.float32)],
        cost_estimate=pl.CostEstimate(
            flops=6 * n * width * (rows.shape[0] + width), bytes_accessed=4 * cov.size, transcendentals=0
        ),
        compiler_params=pltpu.CompilerParams(vmem_limit_bytes=16 << 20),
    )(core.reshape(1), cov, rows, cols)


def invert_kernel(m_ref, noise_ref, out_ref):
    n = m_ref.shape[0]
    eye = lax.broadcasted_iota(jnp.int32, (n, n), 0) == lax.broadcasted_iota(jnp.int32, (n, n), 1)
    one = jnp.where(eye, 1.0, 0.0).astype(jnp.float32)
    system = m_ref[...] + jnp.where(eye, noise_ref[...], 0.0)
    diag = jnp.where(eye, system, 0.0)
    across = lax.rsqrt(jnp.sum(diag, axis=0, keepdims=True))
    down = lax.rsqrt(jnp.sum(diag, axis=1, keepdims=True))
    scaled = system * down * across
    bound = jnp.max(jnp.sum(jnp.abs(scaled), axis=1, keepdims=True), axis=0, keepdims=True)
    alpha = 2.0 / (1.0 + bound)
    err = one - alpha * scaled
    start = alpha * (one + err)

    def fast(a, b):
        return jnp.dot(a.astype(jnp.bfloat16), b.astype(jnp.bfloat16), preferred_element_type=jnp.float32)

    def full(a, b):
        return jnp.dot(a, b, precision=HIGHEST, preferred_element_type=jnp.float32)

    err2 = fast(err, err)
    err4 = fast(err2, err2)
    guess = start + fast(start, err2)
    guess = guess + fast(guess, err4)

    def norm(r):
        return jnp.max(jnp.sum(jnp.abs(r), axis=0, keepdims=True))

    rest = one - full(scaled, guess)
    size = norm(rest)
    bad = size >= 0.5
    guess = jnp.where(bad, start, guess)

    def go_on(state):
        return jnp.logical_and(state[1] >= 1e-3, state[2] < 60)

    def refine(state):
        y = state[0]
        r = one - full(scaled, y)
        return y + full(y, r), norm(r), state[2] + 1

    guess, _, _ = lax.while_loop(go_on, refine, (guess, jnp.float32(1.0), jnp.int32(0)))
    out_ref[...] = guess * down * across


def inverse_of(m, noise):
    n = m.shape[0]
    return pl.pallas_call(
        invert_kernel,
        out_shape=jax.ShapeDtypeStruct((n, n), jnp.float32),
        cost_estimate=pl.CostEstimate(flops=2 * n**3 * 40, bytes_accessed=4 * n * n * 3, transcendentals=n),
        compiler_params=pltpu.CompilerParams(vmem_limit_bytes=4 << 20),
    )(m, noise)


def step(covariance, features, noise):
    r = lax.axis_index("row")
    z, core = r >> 1, r & 1
    steps, block, batch = features.shape
    width = steps * batch
    own = jnp.moveaxis(features, 0, 1).reshape(block, width)
    turned = covariance.T

    row_features = to_plane(own)
    apart = to_place(own, feature_place)
    za = side(apart, to_xor(apart, "row", 2), z & 1)
    zb = side(za, to_xor(za, "row", 6), z >> 1)
    column_features = side(zb, to_xor(zb, "row", 1), core).reshape(8 * block, width)

    kept, given = products(core, turned, row_features, column_features)
    mate = to_xor(given, "row", 1)

    def part(d):
        return lax.dynamic_index_in_dim(kept, z ^ d, 0, keepdims=False) + lax.dynamic_index_in_dim(
            mate, z ^ d, 0, keepdims=False
        )

    arrived = [to_xor(part(d), "row", 2 * d) for d in (2, 1, 3)]
    total = (part(0) + arrived[0]) + (arrived[1] + arrived[2])
    product, share = total[:block], total[block:]

    for bits in (1, 3, 4, 12):
        share = share + to_xor(share, "col", bits)
    shares = side(share, to_xor(share, "row", 2), z & 1)
    shares = side(shares, to_xor(shares, "row", 6), z >> 1)
    matrix = side(shares, to_xor(shares, "row", 1), core).reshape(width, width)

    cols = side(product, to_xor(product, "row", 2), z & 1)
    cols = side(cols, to_xor(cols, "row", 6), z >> 1)
    product_cols = side(cols, to_xor(cols, "row", 1), core).reshape(8 * block, width)

    product_rows = to_plane(to_place(product, product_place))

    inverse = inverse_of(matrix, noise.reshape(1, width))
    gain = dot(product_cols, inverse, ((1,), (0,)), HIGH)
    return (turned - dot(gain, product_rows, ((1,), (1,)), HIGH)).T


def solution(mesh):
    specs = (P("row", "col"), P(None, ("row", "col"), None), P())
    return jax.shard_map(step, mesh=mesh, in_specs=specs, out_specs=P("row", "col"), check_vma=False)
```

```python
import jax
import jax.numpy as jnp
from jax import lax
from jax.experimental import pallas as pl
from jax.experimental.pallas import tpu as pltpu
from jax.sharding import PartitionSpec as P


HIGHEST = lax.Precision.HIGHEST
HIGH = lax.Precision.HIGH


def to_xor(value, axis, bits):
    size = lax.axis_size(axis)
    return lax.ppermute(value, axis, [(i, i ^ bits) for i in range(size)])


def to_place(value, owner):
    return lax.ppermute(value, ("row", "col"), [(i, owner(i)) for i in range(128)])


def side(a, b, bit):
    first = jnp.where(bit == 0, a, b)
    second = jnp.where(bit == 0, b, a)
    return jnp.stack([first, second])


def feature_place(index):
    col, part = index // 8, index % 8
    return (2 * (part % 4) + part // 4) * 16 + col


def product_place(index):
    row, col = index // 16, index % 16
    return 8 * col + 4 * (row % 2) + row // 2


def to_plane(block):
    devices = lax.axis_size("col")
    sent = jnp.broadcast_to(block[None], (devices, *block.shape))
    return lax.all_to_all(sent, "col", 0, 0, tiled=True).reshape(-1, block.shape[-1])


def halves(a):
    high = a.astype(jnp.bfloat16)
    return high, (a - high.astype(jnp.float32)).astype(jnp.bfloat16)


def near_full(a, b, dims):
    (ah, al), (bh, bl) = a, b
    dims = (dims, ((), ()))

    def one(p, q):
        return lax.dot_general(p, q, dims, preferred_element_type=jnp.float32)

    return one(ah, bh) + (one(ah, bl) + one(al, bh))


def products_kernel(core_ref, cov_ref, rows_ref, own_ref, other_ref, kept_ref, given_ref, t_ref, m_ref, cols_ref):
    core = core_ref[0]
    block, share = t_ref.shape[0] // 8, m_ref.shape[0] // 8
    cut = 2 * block
    right = halves(rows_ref[...])
    cols_ref[pl.ds(pl.multiple_of(core * 4 * block, 8), 4 * block), :] = own_ref[...]
    cols_ref[pl.ds(pl.multiple_of((1 - core) * 4 * block, 8), 4 * block), :] = other_ref[...]
    for i in range(4):
        t_ref[pl.ds(i * cut, cut), :] = near_full(halves(cov_ref[pl.ds(i * cut, cut), :]), right, ((1,), (0,)))
    m_ref[...] = near_full(halves(cols_ref[...]), halves(t_ref[...]), ((0,), (0,)))
    for ref, at in ((kept_ref, core), (given_ref, 1 - core)):
        for i in range(4):
            ref[i, :block, :] = t_ref[pl.ds(pl.multiple_of((4 * at + i) * block, 8), block), :]
            ref[i, block:, :] = m_ref[pl.ds(pl.multiple_of((4 * at + i) * share, 8), share), :]


SCALAR = pl.BlockSpec(memory_space=pltpu.SMEM)
VMEM = pl.BlockSpec(memory_space=pltpu.VMEM)


def products(core, cov, rows, own, other):
    n, width = 2 * own.shape[0], own.shape[1]
    depth = n // 8 + width // 8
    exchange = pltpu.VMEM((4, depth, width), jnp.float32)
    return pl.pallas_call(
        products_kernel,
        out_shape=(exchange, exchange),
        in_specs=[SCALAR, VMEM, VMEM, VMEM, VMEM],
        out_specs=(VMEM, VMEM),
        scratch_shapes=[
            pltpu.VMEM((n, width), jnp.float32),
            pltpu.VMEM((width, width), jnp.float32),
            pltpu.VMEM((n, width), jnp.float32),
        ],
        cost_estimate=pl.CostEstimate(
            flops=6 * n * width * (rows.shape[0] + width), bytes_accessed=4 * cov.size, transcendentals=0
        ),
        compiler_params=pltpu.CompilerParams(vmem_limit_bytes=20 << 20),
    )(core.reshape(1), cov, rows, own, other)


def pieces_kernel(z_ref, kept_ref, mate_ref, *out_refs):
    for d, ref in enumerate(out_refs):
        at = z_ref[0] ^ d
        ref[...] = kept_ref[at] + mate_ref[at]


def pieces(z, kept, mate):
    piece = pltpu.VMEM(kept.shape[1:], jnp.float32)
    return pl.pallas_call(
        pieces_kernel,
        out_shape=(piece,) * 4,
        in_specs=[SCALAR, VMEM, VMEM],
        out_specs=(VMEM,) * 4,
        compiler_params=pltpu.CompilerParams(vmem_limit_bytes=4 << 20),
    )(z.reshape(1), kept, mate)


def total_kernel(a_ref, b_ref, c_ref, d_ref, product_ref, share_ref):
    total = (a_ref[...] + b_ref[...]) + (c_ref[...] + d_ref[...])
    product_ref[...] = total[: product_ref.shape[0]]
    share_ref[...] = total[product_ref.shape[0] :]


def totals(terms, block):
    depth, width = terms[0].shape
    return pl.pallas_call(
        total_kernel,
        out_shape=(pltpu.VMEM((block, width), jnp.float32), pltpu.VMEM((depth - block, width), jnp.float32)),
        in_specs=[VMEM] * 4,
        out_specs=(VMEM, VMEM),
        compiler_params=pltpu.CompilerParams(vmem_limit_bytes=4 << 20),
    )(*terms)


def gain_kernel(core_ref, own_ref, other_ref, inv_ref, out_ref):
    core, half = core_ref[0], own_ref.shape[0]
    inverse = halves(inv_ref[...])
    for ref, at in ((own_ref, core), (other_ref, 1 - core)):
        out_ref[pl.ds(pl.multiple_of(at * half, 8), half), :] = near_full(halves(ref[...]), inverse, ((1,), (0,)))


def gain_of(core, own, other, inverse):
    return pl.pallas_call(
        gain_kernel,
        out_shape=pltpu.VMEM((2 * own.shape[0], own.shape[1]), jnp.float32),
        in_specs=[SCALAR, VMEM, VMEM, VMEM],
        out_specs=VMEM,
        compiler_params=pltpu.CompilerParams(vmem_limit_bytes=6 << 20),
    )(core.reshape(1), own, other, inverse)


def hold_kernel(far_ref, near_ref, sems):
    cut = near_ref.shape[0] // 4
    copies = [
        pltpu.make_async_copy(far_ref.at[pl.ds(i * cut, cut)], near_ref.at[pl.ds(i * cut, cut)], sems.at[i])
        for i in range(4)
    ]
    for copy in copies:
        copy.start()
    for copy in copies:
        copy.wait()


def hold(cov):
    cov = pltpu.with_memory_space_constraint(cov, pltpu.HBM)
    return pl.pallas_call(
        hold_kernel,
        out_shape=pltpu.VMEM(cov.shape, jnp.float32),
        in_specs=[pl.BlockSpec(memory_space=pltpu.HBM)],
        out_specs=VMEM,
        scratch_shapes=[pltpu.SemaphoreType.DMA((4,))],
        compiler_params=pltpu.CompilerParams(vmem_limit_bytes=4 << 20),
    )(cov)


def invert_kernel(m_ref, noise_ref, out_ref):
    n = m_ref.shape[0]
    eye = lax.broadcasted_iota(jnp.int32, (n, n), 0) == lax.broadcasted_iota(jnp.int32, (n, n), 1)
    one = jnp.where(eye, 1.0, 0.0).astype(jnp.float32)
    system = m_ref[...] + jnp.where(eye, noise_ref[...], 0.0)
    diag = jnp.where(eye, system, 0.0)
    across = lax.rsqrt(jnp.sum(diag, axis=0, keepdims=True))
    down = lax.rsqrt(jnp.sum(diag, axis=1, keepdims=True))
    scaled = system * down * across
    bound = jnp.max(jnp.sum(jnp.abs(scaled), axis=1, keepdims=True), axis=0, keepdims=True)
    alpha = 2.0 / (1.0 + bound)
    err = one - alpha * scaled
    start = alpha * (one + err)

    def fast(a, b):
        return jnp.dot(a.astype(jnp.bfloat16), b.astype(jnp.bfloat16), preferred_element_type=jnp.float32)

    def full(a, b):
        return jnp.dot(a, b, precision=HIGHEST, preferred_element_type=jnp.float32)

    err2 = fast(err, err)
    err4 = fast(err2, err2)
    guess = start + fast(start, err2)
    guess = guess + fast(guess, err4)

    def norm(r):
        return jnp.max(jnp.sum(jnp.abs(r), axis=0, keepdims=True))

    rest = one - full(scaled, guess)
    size = norm(rest)
    slow = size >= 0.5

    def go_on(state):
        return jnp.logical_and(state[2] >= 1e-3, state[3] < 60)

    def refine(state):
        y, r, _, count = state
        y = y + full(y, r)
        r = one - full(scaled, y)
        return y, r, norm(r), count + 1

    guess, rest = lax.cond(
        slow, lambda: (start, one - full(scaled, start)), lambda: (guess, rest)
    )
    guess, rest, _, _ = lax.while_loop(go_on, refine, (guess, rest, size, jnp.int32(0)))
    guess = guess + full(guess, rest)
    out_ref[...] = guess * down * across


def inverse_of(m, noise):
    n = m.shape[0]
    return pl.pallas_call(
        invert_kernel,
        out_shape=jax.ShapeDtypeStruct((n, n), jnp.float32),
        cost_estimate=pl.CostEstimate(flops=2 * n**3 * 40, bytes_accessed=4 * n * n * 3, transcendentals=n),
        compiler_params=pltpu.CompilerParams(vmem_limit_bytes=4 << 20),
    )(m, noise)


def step(covariance, features, noise):
    r = lax.axis_index("row")
    z, core = r >> 1, r & 1
    steps, block, batch = features.shape
    width = steps * batch
    own = jnp.moveaxis(features, 0, 1).reshape(block, width)
    turned = hold(covariance.T)

    row_features = to_plane(own)
    apart = to_place(own, feature_place)
    za = side(apart, to_xor(apart, "row", 2), z & 1)
    zb = side(za, to_xor(za, "row", 6), z >> 1)
    quad = zb.reshape(4 * block, width)

    kept, given = products(core, turned, row_features, quad, to_xor(quad, "row", 1))
    terms = pieces(z, kept, to_xor(given, "row", 1))
    product, share = totals([terms[0]] + [to_xor(terms[d], "row", 2 * d) for d in (1, 2, 3)], block)

    for bits in (1, 3, 4, 12):
        share = share + to_xor(share, "col", bits)
    shares = side(share, to_xor(share, "row", 2), z & 1)
    shares = side(shares, to_xor(shares, "row", 6), z >> 1)
    matrix = side(shares, to_xor(shares, "row", 1), core).reshape(width, width)

    cols = side(product, to_xor(product, "row", 2), z & 1)
    cols = side(cols, to_xor(cols, "row", 6), z >> 1).reshape(4 * block, width)
    other_cols = to_xor(cols, "row", 1)

    product_rows = to_plane(to_place(product, product_place))

    inverse = inverse_of(matrix, noise.reshape(1, width))
    gain = gain_of(core, cols, other_cols, inverse)
    product_rows = hold(product_rows)
    change = lax.dot_general(
        gain, product_rows, (((1,), (1,)), ((), ())), precision=HIGH, preferred_element_type=jnp.float32
    )
    return (turned - change).T


def solution(mesh):
    specs = (P("row", "col"), P(None, ("row", "col"), None), P())
    return jax.shard_map(step, mesh=mesh, in_specs=specs, out_specs=P("row", "col"), check_vma=False)
```

```python
import jax
import jax.numpy as jnp
from jax import lax
from jax.experimental import pallas as pl
from jax.experimental.pallas import tpu as pltpu
from jax.sharding import PartitionSpec as P


HIGHEST = lax.Precision.HIGHEST
HIGH = lax.Precision.HIGH


def to_xor(value, axis, bits):
    size = lax.axis_size(axis)
    return lax.ppermute(value, axis, [(i, i ^ bits) for i in range(size)])


def to_place(value, owner):
    return lax.ppermute(value, ("row", "col"), [(i, owner(i)) for i in range(128)])


def side(a, b, bit):
    first = jnp.where(bit == 0, a, b)
    second = jnp.where(bit == 0, b, a)
    return jnp.stack([first, second])


def feature_place(index):
    col, part = index // 8, index % 8
    return (2 * (part % 4) + part // 4) * 16 + col


def product_place(index):
    row, col = index // 16, index % 16
    return 8 * col + 4 * (row % 2) + row // 2


def to_plane(block):
    devices = lax.axis_size("col")
    sent = jnp.broadcast_to(block[None], (devices, *block.shape))
    return lax.all_to_all(sent, "col", 0, 0, tiled=True).reshape(-1, block.shape[-1])


def halves(a):
    high = a.astype(jnp.bfloat16)
    return high, (a - high.astype(jnp.float32)).astype(jnp.bfloat16)


def near_full(a, b, dims):
    (ah, al), (bh, bl) = a, b
    dims = (dims, ((), ()))

    def one(p, q):
        return lax.dot_general(p, q, dims, preferred_element_type=jnp.float32)

    return one(ah, bh) + (one(ah, bl) + one(al, bh))


def products_kernel(core_ref, cov_ref, rows_ref, own_ref, other_ref, kept_ref, given_ref, t_ref, m_ref, cols_ref):
    core = core_ref[0]
    block, share = t_ref.shape[0] // 8, m_ref.shape[0] // 8
    cut = 2 * block
    right = halves(rows_ref[...])
    cols_ref[pl.ds(pl.multiple_of(core * 4 * block, 8), 4 * block), :] = own_ref[...]
    cols_ref[pl.ds(pl.multiple_of((1 - core) * 4 * block, 8), 4 * block), :] = other_ref[...]
    for i in range(4):
        t_ref[pl.ds(i * cut, cut), :] = near_full(halves(cov_ref[pl.ds(i * cut, cut), :]), right, ((1,), (0,)))
    m_ref[...] = near_full(halves(cols_ref[...]), halves(t_ref[...]), ((0,), (0,)))
    for ref, at in ((kept_ref, core), (given_ref, 1 - core)):
        for i in range(4):
            ref[i, :block, :] = t_ref[pl.ds(pl.multiple_of((4 * at + i) * block, 8), block), :]
            ref[i, block:, :] = m_ref[pl.ds(pl.multiple_of((4 * at + i) * share, 8), share), :]


SCALAR = pl.BlockSpec(memory_space=pltpu.SMEM)
VMEM = pl.BlockSpec(memory_space=pltpu.VMEM)


def products(core, cov, rows, own, other):
    n, width = 2 * own.shape[0], own.shape[1]
    depth = n // 8 + width // 8
    exchange = pltpu.VMEM((4, depth, width), jnp.float32)
    return pl.pallas_call(
        products_kernel,
        out_shape=(exchange, exchange),
        in_specs=[SCALAR, VMEM, VMEM, VMEM, VMEM],
        out_specs=(VMEM, VMEM),
        scratch_shapes=[
            pltpu.VMEM((n, width), jnp.float32),
            pltpu.VMEM((width, width), jnp.float32),
            pltpu.VMEM((n, width), jnp.float32),
        ],
        cost_estimate=pl.CostEstimate(
            flops=6 * n * width * (rows.shape[0] + width), bytes_accessed=4 * cov.size, transcendentals=0
        ),
        compiler_params=pltpu.CompilerParams(vmem_limit_bytes=20 << 20),
    )(core.reshape(1), cov, rows, own, other)


def pieces_kernel(z_ref, kept_ref, mate_ref, *out_refs):
    for d, ref in enumerate(out_refs):
        at = z_ref[0] ^ d
        ref[...] = kept_ref[at] + mate_ref[at]


def pieces(z, kept, mate):
    piece = pltpu.VMEM(kept.shape[1:], jnp.float32)
    return pl.pallas_call(
        pieces_kernel,
        out_shape=(piece,) * 4,
        in_specs=[SCALAR, VMEM, VMEM],
        out_specs=(VMEM,) * 4,
        compiler_params=pltpu.CompilerParams(vmem_limit_bytes=4 << 20),
    )(z.reshape(1), kept, mate)


def total_kernel(a_ref, b_ref, c_ref, d_ref, product_ref, share_ref):
    total = (a_ref[...] + b_ref[...]) + (c_ref[...] + d_ref[...])
    product_ref[...] = total[: product_ref.shape[0]]
    share_ref[...] = total[product_ref.shape[0] :]


def totals(terms, block):
    depth, width = terms[0].shape
    return pl.pallas_call(
        total_kernel,
        out_shape=(pltpu.VMEM((block, width), jnp.float32), pltpu.VMEM((depth - block, width), jnp.float32)),
        in_specs=[VMEM] * 4,
        out_specs=(VMEM, VMEM),
        compiler_params=pltpu.CompilerParams(vmem_limit_bytes=4 << 20),
    )(*terms)


def pack_kernel(z_ref, cols_ref, far_cols_ref, *refs):
    out_ref = refs[-1]
    z = z_ref[0]
    block = cols_ref.shape[1]
    for half, cols in ((0, cols_ref), (1, far_cols_ref)):
        for j in range(2):
            out_ref[2 * ((z >> 1) ^ half) + j, :block, :] = cols[j]
    for d, share in enumerate(refs[:-1]):
        out_ref[z ^ d, block:, :] = share[...]


def pack(z, cols, far_cols, shares):
    depth = cols.shape[1] + shares[0].shape[0]
    return pl.pallas_call(
        pack_kernel,
        out_shape=pltpu.VMEM((4, depth, cols.shape[2]), jnp.float32),
        in_specs=[SCALAR] + [VMEM] * 6,
        out_specs=VMEM,
        compiler_params=pltpu.CompilerParams(vmem_limit_bytes=4 << 20),
    )(z.reshape(1), cols, far_cols, *shares)


def gain_kernel(core_ref, own_ref, other_ref, inv_ref, out_ref):
    block = out_ref.shape[0] // 8
    inverse = halves(inv_ref[...])
    for ref, at in ((own_ref, core_ref[0]), (other_ref, 1 - core_ref[0])):
        for j in range(4):
            out_ref[pl.ds(pl.multiple_of((4 * at + j) * block, 8), block), :] = ref[j, :block, :]
    out_ref[...] = near_full(halves(out_ref[...]), inverse, ((1,), (0,)))


def gain_of(core, own, other, inverse, block):
    return pl.pallas_call(
        gain_kernel,
        out_shape=pltpu.VMEM((8 * block, own.shape[2]), jnp.float32),
        in_specs=[SCALAR, VMEM, VMEM, VMEM],
        out_specs=VMEM,
        compiler_params=pltpu.CompilerParams(vmem_limit_bytes=6 << 20),
    )(core.reshape(1), own, other, inverse)


def hold_kernel(far_ref, near_ref, sems):
    cut = near_ref.shape[0] // 4
    copies = [
        pltpu.make_async_copy(far_ref.at[pl.ds(i * cut, cut)], near_ref.at[pl.ds(i * cut, cut)], sems.at[i])
        for i in range(4)
    ]
    for copy in copies:
        copy.start()
    for copy in copies:
        copy.wait()


def hold(cov):
    cov = pltpu.with_memory_space_constraint(cov, pltpu.HBM)
    return pl.pallas_call(
        hold_kernel,
        out_shape=pltpu.VMEM(cov.shape, jnp.float32),
        in_specs=[pl.BlockSpec(memory_space=pltpu.HBM)],
        out_specs=VMEM,
        scratch_shapes=[pltpu.SemaphoreType.DMA((4,))],
        compiler_params=pltpu.CompilerParams(vmem_limit_bytes=4 << 20),
    )(cov)


def invert_kernel(core_ref, own_ref, other_ref, noise_ref, out_ref, m_ref):
    n = m_ref.shape[0]
    share = n // 8
    for ref, at in ((own_ref, core_ref[0]), (other_ref, 1 - core_ref[0])):
        for j in range(4):
            m_ref[pl.ds(pl.multiple_of((4 * at + j) * share, 8), share), :] = ref[j, ref.shape[1] - share :, :]
    eye = lax.broadcasted_iota(jnp.int32, (n, n), 0) == lax.broadcasted_iota(jnp.int32, (n, n), 1)
    one = jnp.where(eye, 1.0, 0.0).astype(jnp.float32)
    system = m_ref[...] + jnp.where(eye, noise_ref[...], 0.0)
    diag = jnp.where(eye, system, 0.0)
    across = lax.rsqrt(jnp.sum(diag, axis=0, keepdims=True))
    down = lax.rsqrt(jnp.sum(diag, axis=1, keepdims=True))
    scaled = system * down * across
    bound = jnp.max(jnp.sum(jnp.abs(scaled), axis=1, keepdims=True), axis=0, keepdims=True)
    alpha = 2.0 / (1.0 + bound)
    err = one - alpha * scaled
    start = alpha * (one + err)

    def fast(a, b):
        return jnp.dot(a.astype(jnp.bfloat16), b.astype(jnp.bfloat16), preferred_element_type=jnp.float32)

    def full(a, b):
        return jnp.dot(a, b, precision=HIGHEST, preferred_element_type=jnp.float32)

    err2 = fast(err, err)
    err4 = fast(err2, err2)
    guess = start + fast(start, err2)
    guess = guess + fast(guess, err4)

    def norm(r):
        return jnp.max(jnp.sum(jnp.abs(r), axis=0, keepdims=True))

    rest = one - full(scaled, guess)
    size = norm(rest)

    def go_on(state):
        return jnp.logical_and(state[2] >= 1e-3, state[3] < 60)

    def finished(multiply, y, r, bound):
        def refine(state):
            y, r, _, count = state
            y = y + multiply(y, r)
            r = one - full(scaled, y)
            return y, r, norm(r), count + 1

        y, r, _, _ = lax.while_loop(go_on, refine, (y, r, bound, jnp.int32(0)))
        return y + multiply(y, r)

    guess = lax.cond(
        size < 0.5,
        lambda: finished(fast, guess, rest, size),
        lambda: finished(full, start, one - full(scaled, start), jnp.float32(1.0)),
    )
    out_ref[...] = guess * down * across


def inverse_of(core, own, other, noise):
    n = noise.shape[1]
    return pl.pallas_call(
        invert_kernel,
        out_shape=pltpu.VMEM((n, n), jnp.float32),
        in_specs=[SCALAR, VMEM, VMEM, VMEM],
        out_specs=VMEM,
        scratch_shapes=[pltpu.VMEM((n, n), jnp.float32)],
        cost_estimate=pl.CostEstimate(flops=2 * n**3 * 40, bytes_accessed=4 * n * n * 3, transcendentals=n),
        compiler_params=pltpu.CompilerParams(vmem_limit_bytes=12 << 20),
    )(core.reshape(1), own, other, noise)


def step(covariance, features, noise):
    r = lax.axis_index("row")
    z, core = r >> 1, r & 1
    steps, block, batch = features.shape
    width = steps * batch
    own = jnp.moveaxis(features, 0, 1).reshape(block, width)
    turned = hold(covariance.T)

    row_features = to_plane(own)
    apart = to_place(own, feature_place)
    za = side(apart, to_xor(apart, "row", 2), z & 1)
    zb = side(za, to_xor(za, "row", 6), z >> 1)
    quad = zb.reshape(4 * block, width)

    kept, given = products(core, turned, row_features, quad, to_xor(quad, "row", 1))
    terms = pieces(z, kept, to_xor(given, "row", 1))
    product, share = totals([terms[0]] + [to_xor(terms[d], "row", 2 * d) for d in (1, 2, 3)], block)

    for unit in (1, 4):
        a, b, c = (to_xor(share, "col", d * unit) for d in (2, 1, 3))
        share = (share + a) + (b + c)
    shares = [share] + [to_xor(share, "row", 2 * d) for d in (1, 2, 3)]
    cols = side(product, to_xor(product, "row", 2), z & 1)
    packed = pack(z, cols, to_xor(cols, "row", 6), shares)
    mate = to_xor(packed, "row", 1)

    product_rows = to_plane(to_place(product, product_place))

    inverse = inverse_of(core, packed, mate, noise.reshape(1, width))
    gain = gain_of(core, packed, mate, inverse, block)
    product_rows = hold(product_rows)
    change = lax.dot_general(
        gain, product_rows, (((1,), (1,)), ((), ())), precision=HIGH, preferred_element_type=jnp.float32
    )
    return (turned - change).T


def solution(mesh):
    specs = (P("row", "col"), P(None, ("row", "col"), None), P())
    return jax.shard_map(step, mesh=mesh, in_specs=specs, out_specs=P("row", "col"), check_vma=False)
```

```python
import jax
import jax.numpy as jnp
from jax import lax
from jax.experimental import pallas as pl
from jax.experimental.pallas import tpu as pltpu
from jax.sharding import PartitionSpec as P


HIGHEST = lax.Precision.HIGHEST


def to_xor(value, axis, bits):
    size = lax.axis_size(axis)
    return lax.ppermute(value, axis, [(i, i ^ bits) for i in range(size)])


def to_place(value, owner):
    return lax.ppermute(value, ("row", "col"), [(i, owner(i)) for i in range(128)])


def side(a, b, bit):
    first = jnp.where(bit == 0, a, b)
    second = jnp.where(bit == 0, b, a)
    return jnp.stack([first, second])


def feature_place(index):
    col, part = index // 8, index % 8
    return (2 * (part % 4) + part // 4) * 16 + col


def product_place(index):
    row, col = index // 16, index % 16
    return 8 * col + 4 * (row % 2) + row // 2


def to_plane(block):
    devices = lax.axis_size("col")
    sent = jnp.broadcast_to(block[None], (devices, *block.shape))
    return lax.all_to_all(sent, "col", 0, 0, tiled=True).reshape(-1, block.shape[-1])


def halves(a):
    high = a.astype(jnp.bfloat16)
    return high, (a - high.astype(jnp.float32)).astype(jnp.bfloat16)


def near_full(a, b, dims):
    (ah, al), (bh, bl) = a, b
    dims = (dims, ((), ()))

    def one(p, q):
        return lax.dot_general(p, q, dims, preferred_element_type=jnp.float32)

    return one(ah, bh) + (one(ah, bl) + one(al, bh))


def products_kernel(core_ref, cov_ref, rows_ref, own_ref, other_ref, kept_ref, given_ref, t_ref, m_ref, cols_ref):
    core = core_ref[0]
    block, share = t_ref.shape[0] // 8, m_ref.shape[0] // 8
    cut = 2 * block
    right = halves(rows_ref[...])
    cols_ref[pl.ds(pl.multiple_of(core * 4 * block, 8), 4 * block), :] = own_ref[...]
    cols_ref[pl.ds(pl.multiple_of((1 - core) * 4 * block, 8), 4 * block), :] = other_ref[...]
    for i in range(4):
        t_ref[pl.ds(i * cut, cut), :] = near_full(halves(cov_ref[pl.ds(i * cut, cut), :]), right, ((1,), (0,)))
    m_ref[...] = near_full(halves(cols_ref[...]), halves(t_ref[...]), ((0,), (0,)))
    for ref, at in ((kept_ref, core), (given_ref, 1 - core)):
        for i in range(4):
            ref[i, :block, :] = t_ref[pl.ds(pl.multiple_of((4 * at + i) * block, 8), block), :]
            ref[i, block:, :] = m_ref[pl.ds(pl.multiple_of((4 * at + i) * share, 8), share), :]


SCALAR = pl.BlockSpec(memory_space=pltpu.SMEM)
VMEM = pl.BlockSpec(memory_space=pltpu.VMEM)
FAR = pl.BlockSpec(memory_space=pltpu.HBM)


def products(core, cov, rows, own, other):
    n, width = 2 * own.shape[0], own.shape[1]
    depth = n // 8 + width // 8
    exchange = pltpu.VMEM((4, depth, width), jnp.float32)
    return pl.pallas_call(
        products_kernel,
        out_shape=(exchange, exchange),
        in_specs=[SCALAR, VMEM, VMEM, VMEM, VMEM],
        out_specs=(VMEM, VMEM),
        scratch_shapes=[
            pltpu.VMEM((n, width), jnp.float32),
            pltpu.VMEM((width, width), jnp.float32),
            pltpu.VMEM((n, width), jnp.float32),
        ],
        cost_estimate=pl.CostEstimate(
            flops=6 * n * width * (rows.shape[0] + width), bytes_accessed=4 * cov.size, transcendentals=0
        ),
        compiler_params=pltpu.CompilerParams(vmem_limit_bytes=20 << 20),
    )(core.reshape(1), cov, pltpu.with_memory_space_constraint(rows, pltpu.VMEM), own, other)


def pieces_kernel(z_ref, kept_ref, mate_ref, *out_refs):
    for d, ref in enumerate(out_refs):
        at = z_ref[0] ^ d
        ref[...] = kept_ref[at] + mate_ref[at]


def pieces(z, kept, mate):
    piece = pltpu.VMEM(kept.shape[1:], jnp.float32)
    return pl.pallas_call(
        pieces_kernel,
        out_shape=(piece,) * 4,
        in_specs=[SCALAR, VMEM, VMEM],
        out_specs=(VMEM,) * 4,
        compiler_params=pltpu.CompilerParams(vmem_limit_bytes=4 << 20),
    )(z.reshape(1), kept, mate)


def total_kernel(a_ref, b_ref, c_ref, d_ref, product_ref, share_ref):
    total = (a_ref[...] + b_ref[...]) + (c_ref[...] + d_ref[...])
    product_ref[...] = total[: product_ref.shape[0]]
    share_ref[...] = total[product_ref.shape[0] :]


def totals(terms, block):
    depth, width = terms[0].shape
    return pl.pallas_call(
        total_kernel,
        out_shape=(pltpu.VMEM((block, width), jnp.float32), pltpu.VMEM((depth - block, width), jnp.float32)),
        in_specs=[VMEM] * 4,
        out_specs=(VMEM, VMEM),
        compiler_params=pltpu.CompilerParams(vmem_limit_bytes=4 << 20),
    )(*terms)


def join_kernel(product_ref, a_ref, b_ref, c_ref, d_ref, out_ref):
    block = product_ref.shape[0]
    out_ref[:block, :] = product_ref[...]
    out_ref[block:, :] = (a_ref[...] + b_ref[...]) + (c_ref[...] + d_ref[...])


def join(product, shares):
    depth = product.shape[0] + shares[0].shape[0]
    return pl.pallas_call(
        join_kernel,
        out_shape=pltpu.VMEM((depth, product.shape[1]), jnp.float32),
        in_specs=[VMEM] * 5,
        out_specs=VMEM,
        compiler_params=pltpu.CompilerParams(vmem_limit_bytes=2 << 20),
    )(product, *shares)


def pack_kernel(z_ref, *refs):
    for d, piece in enumerate(refs[:-1]):
        refs[-1][z_ref[0] ^ d] = piece[...]


def pack(z, parts):
    return pl.pallas_call(
        pack_kernel,
        out_shape=pltpu.VMEM((4, *parts[0].shape), jnp.float32),
        in_specs=[SCALAR] + [VMEM] * 4,
        out_specs=VMEM,
        compiler_params=pltpu.CompilerParams(vmem_limit_bytes=4 << 20),
    )(z.reshape(1), *parts)


def columns_kernel(far_ref, own_ref, sems):
    batch = far_ref.shape[2]
    copies = [
        pltpu.make_async_copy(far_ref.at[i], own_ref.at[:, pl.ds(i * batch, batch)], sems.at[i])
        for i in range(far_ref.shape[0])
    ]
    for copy in copies:
        copy.start()
    for copy in copies:
        copy.wait()


def columns_of(features):
    steps, block, batch = features.shape
    return pl.pallas_call(
        columns_kernel,
        out_shape=pltpu.VMEM((block, steps * batch), jnp.float32),
        in_specs=[FAR],
        out_specs=VMEM,
        scratch_shapes=[pltpu.SemaphoreType.DMA((steps,))],
        compiler_params=pltpu.CompilerParams(vmem_limit_bytes=2 << 20),
    )(pltpu.with_memory_space_constraint(features, pltpu.HBM))


def update_kernel(cov_ref, rows_ref, gain_ref, far_ref, out_ref, sems):
    cut = cov_ref.shape[0] // 2
    rows = halves(rows_ref[...])
    copies = []
    for i in range(2):
        at = pl.ds(i * cut, cut)
        out_ref[at, :] = cov_ref[at, :] - near_full(halves(gain_ref[at, :]), rows, ((1,), (1,)))
        copies.append(pltpu.make_async_copy(out_ref.at[at], far_ref.at[at], sems.at[i]))
        copies[-1].start()
    for copy in copies:
        copy.wait()


def update(cov, rows, gain):
    return pl.pallas_call(
        update_kernel,
        out_shape=pltpu.HBM(cov.shape, jnp.float32),
        in_specs=[VMEM, VMEM, VMEM],
        out_specs=FAR,
        scratch_shapes=[pltpu.VMEM(cov.shape, jnp.float32), pltpu.SemaphoreType.DMA((2,))],
        cost_estimate=pl.CostEstimate(
            flops=6 * cov.size * rows.shape[1], bytes_accessed=4 * cov.size, transcendentals=0
        ),
        compiler_params=pltpu.CompilerParams(vmem_limit_bytes=20 << 20),
    )(cov, pltpu.with_memory_space_constraint(rows, pltpu.VMEM), gain)


def gain_kernel(core_ref, own_ref, other_ref, inv_ref, out_ref):
    block = out_ref.shape[0] // 8
    inverse = halves(inv_ref[...])
    for ref, at in ((own_ref, core_ref[0]), (other_ref, 1 - core_ref[0])):
        for j in range(4):
            out_ref[pl.ds(pl.multiple_of((4 * at + j) * block, 8), block), :] = ref[j, :block, :]
    out_ref[...] = near_full(halves(out_ref[...]), inverse, ((1,), (0,)))


def gain_of(core, own, other, inverse, block):
    return pl.pallas_call(
        gain_kernel,
        out_shape=pltpu.VMEM((8 * block, own.shape[2]), jnp.float32),
        in_specs=[SCALAR, VMEM, VMEM, VMEM],
        out_specs=VMEM,
        compiler_params=pltpu.CompilerParams(vmem_limit_bytes=6 << 20),
    )(core.reshape(1), own, other, inverse)


def hold_kernel(far_ref, near_ref, sems):
    cut = near_ref.shape[0] // 4
    copies = [
        pltpu.make_async_copy(far_ref.at[pl.ds(i * cut, cut)], near_ref.at[pl.ds(i * cut, cut)], sems.at[i])
        for i in range(4)
    ]
    for copy in copies:
        copy.start()
    for copy in copies:
        copy.wait()


def hold(cov):
    cov = pltpu.with_memory_space_constraint(cov, pltpu.HBM)
    return pl.pallas_call(
        hold_kernel,
        out_shape=pltpu.VMEM(cov.shape, jnp.float32),
        in_specs=[pl.BlockSpec(memory_space=pltpu.HBM)],
        out_specs=VMEM,
        scratch_shapes=[pltpu.SemaphoreType.DMA((4,))],
        compiler_params=pltpu.CompilerParams(vmem_limit_bytes=4 << 20),
    )(cov)


def invert_kernel(core_ref, own_ref, other_ref, noise_ref, out_ref, m_ref):
    n = m_ref.shape[0]
    share = n // 8
    for ref, at in ((own_ref, core_ref[0]), (other_ref, 1 - core_ref[0])):
        for j in range(4):
            m_ref[pl.ds(pl.multiple_of((4 * at + j) * share, 8), share), :] = ref[j, ref.shape[1] - share :, :]
    eye = lax.broadcasted_iota(jnp.int32, (n, n), 0) == lax.broadcasted_iota(jnp.int32, (n, n), 1)
    one = jnp.where(eye, 1.0, 0.0).astype(jnp.float32)
    system = m_ref[...] + jnp.where(eye, noise_ref[...], 0.0)
    diag = jnp.where(eye, system, 0.0)
    across = lax.rsqrt(jnp.sum(diag, axis=0, keepdims=True))
    down = lax.rsqrt(jnp.sum(diag, axis=1, keepdims=True))
    scaled = system * down * across
    bound = jnp.max(jnp.sum(jnp.abs(scaled), axis=1, keepdims=True), axis=0, keepdims=True)
    alpha = 2.0 / (1.0 + bound)
    err = one - alpha * scaled
    start = alpha * (one + err)

    def fast(a, b):
        return jnp.dot(a.astype(jnp.bfloat16), b.astype(jnp.bfloat16), preferred_element_type=jnp.float32)

    def full(a, b):
        return jnp.dot(a, b, precision=HIGHEST, preferred_element_type=jnp.float32)

    err2 = fast(err, err)
    err4 = fast(err2, err2)
    guess = start + fast(start, err2)
    guess = guess + fast(guess, err4)

    def norm(r):
        return jnp.max(jnp.sum(jnp.abs(r), axis=0, keepdims=True))

    rest = one - full(scaled, guess)
    size = norm(rest)

    def go_on(state):
        return jnp.logical_and(state[2] >= 1e-3, state[3] < 60)

    def finished(multiply, y, r, bound):
        def refine(state):
            y, r, _, count = state
            y = y + multiply(y, r)
            r = one - full(scaled, y)
            return y, r, norm(r), count + 1

        y, r, _, _ = lax.while_loop(go_on, refine, (y, r, bound, jnp.int32(0)))
        return y + multiply(y, r)

    guess = lax.cond(
        size < 0.5,
        lambda: finished(fast, guess, rest, size),
        lambda: finished(full, start, one - full(scaled, start), jnp.float32(1.0)),
    )
    out_ref[...] = guess * down * across


def inverse_of(core, own, other, noise):
    n = noise.shape[1]
    return pl.pallas_call(
        invert_kernel,
        out_shape=pltpu.VMEM((n, n), jnp.float32),
        in_specs=[SCALAR, VMEM, VMEM, VMEM],
        out_specs=VMEM,
        scratch_shapes=[pltpu.VMEM((n, n), jnp.float32)],
        cost_estimate=pl.CostEstimate(flops=2 * n**3 * 40, bytes_accessed=4 * n * n * 3, transcendentals=n),
        compiler_params=pltpu.CompilerParams(vmem_limit_bytes=12 << 20),
    )(core.reshape(1), own, other, noise)


def step(covariance, features, noise):
    r = lax.axis_index("row")
    z, core = r >> 1, r & 1
    steps, block, batch = features.shape
    width = steps * batch
    own = columns_of(features)
    turned = hold(covariance.T)

    row_features = to_plane(own)
    apart = to_place(own, feature_place)
    za = side(apart, to_xor(apart, "row", 2), z & 1)
    zb = side(za, to_xor(za, "row", 6), z >> 1)
    quad = zb.reshape(4 * block, width)

    kept, given = products(core, turned, row_features, quad, to_xor(quad, "row", 1))
    terms = pieces(z, kept, to_xor(given, "row", 1))
    product, share = totals([terms[0]] + [to_xor(terms[d], "row", 2 * d) for d in (1, 2, 3)], block)

    for unit in (1, 4):
        sums = [share] + [to_xor(share, "col", d * unit) for d in (1, 2, 3)]
        share = (sums[0] + sums[1]) + (sums[2] + sums[3])
    joined = join(product, sums)
    packed = pack(z, [joined] + [to_xor(joined, "row", 2 * d) for d in (1, 2, 3)])
    mate = to_xor(packed, "row", 1)

    product_rows = to_plane(to_place(product, product_place))

    inverse = inverse_of(core, packed, mate, noise.reshape(1, width))
    gain = gain_of(core, packed, mate, inverse, block)
    return update(turned, product_rows, gain).T


def solution(mesh):
    specs = (P("row", "col"), P(None, ("row", "col"), None), P())
    return jax.shard_map(step, mesh=mesh, in_specs=specs, out_specs=P("row", "col"), check_vma=False)
```

```python
import jax
import jax.numpy as jnp
from jax import lax
from jax.experimental import pallas as pl
from jax.experimental.pallas import tpu as pltpu
from jax.sharding import PartitionSpec as P


HIGHEST = lax.Precision.HIGHEST


def to_xor(value, axis, bits):
    size = lax.axis_size(axis)
    return lax.ppermute(value, axis, [(i, i ^ bits) for i in range(size)])


def to_place(value, owner):
    return lax.ppermute(value, ("row", "col"), [(i, owner(i)) for i in range(128)])


def side(a, b, bit):
    first = jnp.where(bit == 0, a, b)
    second = jnp.where(bit == 0, b, a)
    return jnp.stack([first, second])


def feature_place(index):
    col, part = index // 8, index % 8
    return (2 * (part % 4) + part // 4) * 16 + col


def product_place(index):
    row, col = index // 16, index % 16
    return 8 * col + 4 * (row % 2) + row // 2


def to_plane(block):
    devices = lax.axis_size("col")
    sent = jnp.broadcast_to(block[None], (devices, *block.shape))
    return lax.all_to_all(sent, "col", 0, 0, tiled=True).reshape(-1, block.shape[-1])


def halves(a):
    high = a.astype(jnp.bfloat16)
    return high, (a - high.astype(jnp.float32)).astype(jnp.bfloat16)


def near_full(a, b, dims):
    (ah, al), (bh, bl) = a, b
    dims = (dims, ((), ()))

    def one(p, q):
        return lax.dot_general(p, q, dims, preferred_element_type=jnp.float32)

    return one(ah, bh) + (one(ah, bl) + one(al, bh))


def products_kernel(core_ref, cov_ref, rows_ref, own_ref, other_ref, kept_ref, given_ref, t_ref, m_ref, cols_ref):
    core = core_ref[0]
    block, share = t_ref.shape[0] // 8, m_ref.shape[0] // 8
    cut = 2 * block
    right = halves(rows_ref[...])
    cols_ref[pl.ds(pl.multiple_of(core * 4 * block, 8), 4 * block), :] = own_ref[...]
    cols_ref[pl.ds(pl.multiple_of((1 - core) * 4 * block, 8), 4 * block), :] = other_ref[...]
    for i in range(4):
        t_ref[pl.ds(i * cut, cut), :] = near_full(halves(cov_ref[pl.ds(i * cut, cut), :]), right, ((1,), (0,)))
    m_ref[...] = near_full(halves(cols_ref[...]), halves(t_ref[...]), ((0,), (0,)))
    for ref, at in ((kept_ref, core), (given_ref, 1 - core)):
        for i in range(4):
            ref[i, :block, :] = t_ref[pl.ds(pl.multiple_of((4 * at + i) * block, 8), block), :]
            ref[i, block:, :] = m_ref[pl.ds(pl.multiple_of((4 * at + i) * share, 8), share), :]


SCALAR = pl.BlockSpec(memory_space=pltpu.SMEM)
VMEM = pl.BlockSpec(memory_space=pltpu.VMEM)
FAR = pl.BlockSpec(memory_space=pltpu.HBM)


def products(core, cov, rows, own, other):
    n, width = 2 * own.shape[0], own.shape[1]
    depth = n // 8 + width // 8
    exchange = pltpu.VMEM((4, depth, width), jnp.float32)
    return pl.pallas_call(
        products_kernel,
        out_shape=(exchange, exchange),
        in_specs=[SCALAR, VMEM, VMEM, VMEM, VMEM],
        out_specs=(VMEM, VMEM),
        scratch_shapes=[
            pltpu.VMEM((n, width), jnp.float32),
            pltpu.VMEM((width, width), jnp.float32),
            pltpu.VMEM((n, width), jnp.float32),
        ],
        cost_estimate=pl.CostEstimate(
            flops=6 * n * width * (rows.shape[0] + width), bytes_accessed=4 * cov.size, transcendentals=0
        ),
        compiler_params=pltpu.CompilerParams(vmem_limit_bytes=20 << 20),
    )(core.reshape(1), cov, pltpu.with_memory_space_constraint(rows, pltpu.VMEM), own, other)


def pieces_kernel(z_ref, kept_ref, mate_ref, *out_refs):
    block = out_refs[0].shape[0]
    for d in range(4):
        at = z_ref[0] ^ d
        out_refs[d][...] = kept_ref[at, :block, :] + mate_ref[at, :block, :]
        out_refs[4 + d][...] = kept_ref[at, block:, :] + mate_ref[at, block:, :]


def pieces(z, kept, mate, block):
    _, depth, width = kept.shape
    product = pltpu.VMEM((block, width), jnp.float32)
    share = pltpu.VMEM((depth - block, width), jnp.float32)
    out = pl.pallas_call(
        pieces_kernel,
        out_shape=(product,) * 4 + (share,) * 4,
        in_specs=[SCALAR, VMEM, VMEM],
        out_specs=(VMEM,) * 8,
        compiler_params=pltpu.CompilerParams(vmem_limit_bytes=4 << 20),
    )(z.reshape(1), kept, mate)
    return out[:4], out[4:]


def total_kernel(a_ref, b_ref, c_ref, d_ref, out_ref):
    out_ref[...] = (a_ref[...] + b_ref[...]) + (c_ref[...] + d_ref[...])


def total_of(terms):
    return pl.pallas_call(
        total_kernel,
        out_shape=pltpu.VMEM(terms[0].shape, jnp.float32),
        in_specs=[VMEM] * 4,
        out_specs=VMEM,
        compiler_params=pltpu.CompilerParams(vmem_limit_bytes=2 << 20),
    )(*terms)


def join_kernel(product_ref, a_ref, b_ref, c_ref, d_ref, out_ref):
    block = product_ref.shape[0]
    out_ref[:block, :] = product_ref[...]
    out_ref[block:, :] = (a_ref[...] + b_ref[...]) + (c_ref[...] + d_ref[...])


def join(product, shares):
    depth = product.shape[0] + shares[0].shape[0]
    return pl.pallas_call(
        join_kernel,
        out_shape=pltpu.VMEM((depth, product.shape[1]), jnp.float32),
        in_specs=[VMEM] * 5,
        out_specs=VMEM,
        compiler_params=pltpu.CompilerParams(vmem_limit_bytes=2 << 20),
    )(product, *shares)


def pack_kernel(z_ref, *refs):
    for d, piece in enumerate(refs[:-1]):
        refs[-1][z_ref[0] ^ d] = piece[...]


def pack(z, parts):
    return pl.pallas_call(
        pack_kernel,
        out_shape=pltpu.VMEM((4, *parts[0].shape), jnp.float32),
        in_specs=[SCALAR] + [VMEM] * 4,
        out_specs=VMEM,
        compiler_params=pltpu.CompilerParams(vmem_limit_bytes=4 << 20),
    )(z.reshape(1), *parts)


def columns_kernel(far_ref, own_ref, sems):
    batch = far_ref.shape[2]
    copies = [
        pltpu.make_async_copy(far_ref.at[i], own_ref.at[:, pl.ds(i * batch, batch)], sems.at[i])
        for i in range(far_ref.shape[0])
    ]
    for copy in copies:
        copy.start()
    for copy in copies:
        copy.wait()


def columns_of(features):
    steps, block, batch = features.shape
    return pl.pallas_call(
        columns_kernel,
        out_shape=pltpu.VMEM((block, steps * batch), jnp.float32),
        in_specs=[FAR],
        out_specs=VMEM,
        scratch_shapes=[pltpu.SemaphoreType.DMA((steps,))],
        compiler_params=pltpu.CompilerParams(vmem_limit_bytes=2 << 20),
    )(pltpu.with_memory_space_constraint(features, pltpu.HBM))


def update_kernel(cov_ref, rows_ref, gain_ref, far_ref, out_ref, sems):
    cut = cov_ref.shape[0] // 2
    rows = halves(rows_ref[...])
    copies = []
    for i in range(2):
        at = pl.ds(i * cut, cut)
        out_ref[at, :] = cov_ref[at, :] - near_full(halves(gain_ref[at, :]), rows, ((1,), (1,)))
        copies.append(pltpu.make_async_copy(out_ref.at[at], far_ref.at[at], sems.at[i]))
        copies[-1].start()
    for copy in copies:
        copy.wait()


def update(cov, rows, gain):
    return pl.pallas_call(
        update_kernel,
        out_shape=pltpu.HBM(cov.shape, jnp.float32),
        in_specs=[VMEM, VMEM, VMEM],
        out_specs=FAR,
        scratch_shapes=[pltpu.VMEM(cov.shape, jnp.float32), pltpu.SemaphoreType.DMA((2,))],
        cost_estimate=pl.CostEstimate(
            flops=6 * cov.size * rows.shape[1], bytes_accessed=4 * cov.size, transcendentals=0
        ),
        compiler_params=pltpu.CompilerParams(vmem_limit_bytes=20 << 20),
    )(cov, pltpu.with_memory_space_constraint(rows, pltpu.VMEM), gain)


def gain_kernel(core_ref, own_ref, other_ref, inv_ref, out_ref):
    block = out_ref.shape[0] // 8
    inverse = halves(inv_ref[...])
    for ref, at in ((own_ref, core_ref[0]), (other_ref, 1 - core_ref[0])):
        for j in range(4):
            out_ref[pl.ds(pl.multiple_of((4 * at + j) * block, 8), block), :] = ref[j, :block, :]
    out_ref[...] = near_full(halves(out_ref[...]), inverse, ((1,), (0,)))


def gain_of(core, own, other, inverse, block):
    return pl.pallas_call(
        gain_kernel,
        out_shape=pltpu.VMEM((8 * block, own.shape[2]), jnp.float32),
        in_specs=[SCALAR, VMEM, VMEM, VMEM],
        out_specs=VMEM,
        compiler_params=pltpu.CompilerParams(vmem_limit_bytes=6 << 20),
    )(core.reshape(1), own, other, inverse)


def hold_kernel(far_ref, near_ref, sems):
    cut = near_ref.shape[0] // 4
    copies = [
        pltpu.make_async_copy(far_ref.at[pl.ds(i * cut, cut)], near_ref.at[pl.ds(i * cut, cut)], sems.at[i])
        for i in range(4)
    ]
    for copy in copies:
        copy.start()
    for copy in copies:
        copy.wait()


def hold(cov):
    cov = pltpu.with_memory_space_constraint(cov, pltpu.HBM)
    return pl.pallas_call(
        hold_kernel,
        out_shape=pltpu.VMEM(cov.shape, jnp.float32),
        in_specs=[pl.BlockSpec(memory_space=pltpu.HBM)],
        out_specs=VMEM,
        scratch_shapes=[pltpu.SemaphoreType.DMA((4,))],
        compiler_params=pltpu.CompilerParams(vmem_limit_bytes=4 << 20),
    )(cov)


def invert_kernel(core_ref, own_ref, other_ref, noise_ref, out_ref, m_ref):
    n = m_ref.shape[0]
    share = n // 8
    for ref, at in ((own_ref, core_ref[0]), (other_ref, 1 - core_ref[0])):
        for j in range(4):
            m_ref[pl.ds(pl.multiple_of((4 * at + j) * share, 8), share), :] = ref[j, ref.shape[1] - share :, :]
    eye = lax.broadcasted_iota(jnp.int32, (n, n), 0) == lax.broadcasted_iota(jnp.int32, (n, n), 1)
    one = jnp.where(eye, 1.0, 0.0).astype(jnp.float32)
    system = m_ref[...] + jnp.where(eye, noise_ref[...], 0.0)
    diag = jnp.where(eye, system, 0.0)
    across = lax.rsqrt(jnp.sum(diag, axis=0, keepdims=True))
    down = lax.rsqrt(jnp.sum(diag, axis=1, keepdims=True))
    scaled = system * down * across
    bound = jnp.max(jnp.sum(jnp.abs(scaled), axis=1, keepdims=True), axis=0, keepdims=True)
    alpha = 2.0 / (1.0 + bound)
    err = one - alpha * scaled
    start = alpha * (one + err)

    def fast(a, b):
        return jnp.dot(a.astype(jnp.bfloat16), b.astype(jnp.bfloat16), preferred_element_type=jnp.float32)

    def full(a, b):
        return jnp.dot(a, b, precision=HIGHEST, preferred_element_type=jnp.float32)

    err2 = fast(err, err)
    err4 = fast(err2, err2)
    guess = start + fast(start, err2)
    guess = guess + fast(guess, err4)

    def norm(r):
        return jnp.max(jnp.sum(jnp.abs(r), axis=0, keepdims=True))

    rest = one - full(scaled, guess)
    size = norm(rest)

    def go_on(state):
        return jnp.logical_and(state[2] >= 1e-3, state[3] < 60)

    def finished(multiply, y, r, bound):
        def refine(state):
            y, r, _, count = state
            y = y + multiply(y, r)
            r = one - full(scaled, y)
            return y, r, norm(r), count + 1

        y, r, _, _ = lax.while_loop(go_on, refine, (y, r, bound, jnp.int32(0)))
        return y + multiply(y, r)

    guess = lax.cond(
        size < 0.5,
        lambda: finished(fast, guess, rest, size),
        lambda: finished(full, start, one - full(scaled, start), jnp.float32(1.0)),
    )
    out_ref[...] = guess * down * across


def inverse_of(core, own, other, noise):
    n = noise.shape[1]
    return pl.pallas_call(
        invert_kernel,
        out_shape=pltpu.VMEM((n, n), jnp.float32),
        in_specs=[SCALAR, VMEM, VMEM, VMEM],
        out_specs=VMEM,
        scratch_shapes=[pltpu.VMEM((n, n), jnp.float32)],
        cost_estimate=pl.CostEstimate(flops=2 * n**3 * 40, bytes_accessed=4 * n * n * 3, transcendentals=n),
        compiler_params=pltpu.CompilerParams(vmem_limit_bytes=12 << 20),
    )(core.reshape(1), own, other, noise)


def step(covariance, features, noise):
    r = lax.axis_index("row")
    z, core = r >> 1, r & 1
    steps, block, batch = features.shape
    width = steps * batch
    own = columns_of(features)
    turned = hold(covariance.T)

    row_features = to_plane(own)
    apart = to_place(own, feature_place)
    za = side(apart, to_xor(apart, "row", 2), z & 1)
    zb = side(za, to_xor(za, "row", 6), z >> 1)
    quad = zb.reshape(4 * block, width)

    kept, given = products(core, turned, row_features, quad, to_xor(quad, "row", 1))
    terms, shares = pieces(z, kept, to_xor(given, "row", 1), block)
    share = total_of([shares[0]] + [to_xor(shares[d], "row", 2 * d) for d in (1, 2, 3)])
    product = total_of([terms[0]] + [to_xor(terms[d], "row", 2 * d) for d in (1, 2, 3)])

    share = total_of([share] + [to_xor(share, "col", d) for d in (1, 2, 3)])
    joined = join(product, [share] + [to_xor(share, "col", 4 * d) for d in (1, 2, 3)])
    packed = pack(z, [joined] + [to_xor(joined, "row", 2 * d) for d in (1, 2, 3)])
    mate = to_xor(packed, "row", 1)

    product_rows = to_plane(to_place(product, product_place))

    inverse = inverse_of(core, packed, mate, noise.reshape(1, width))
    gain = gain_of(core, packed, mate, inverse, block)
    return update(turned, product_rows, gain).T


def solution(mesh):
    specs = (P("row", "col"), P(None, ("row", "col"), None), P())
    return jax.shard_map(step, mesh=mesh, in_specs=specs, out_specs=P("row", "col"), check_vma=False)
```

```python
import jax
import jax.numpy as jnp
from jax import lax
from jax.experimental import pallas as pl
from jax.experimental.pallas import tpu as pltpu
from jax.sharding import PartitionSpec as P


HIGHEST = lax.Precision.HIGHEST


def to_xor(value, axis, bits):
    size = lax.axis_size(axis)
    return lax.ppermute(value, axis, [(i, i ^ bits) for i in range(size)])


def to_place(value, owner):
    return lax.ppermute(value, ("row", "col"), [(i, owner(i)) for i in range(128)])


def side(a, b, bit):
    first = jnp.where(bit == 0, a, b)
    second = jnp.where(bit == 0, b, a)
    return jnp.stack([first, second])


def feature_place(index):
    col, part = index // 8, index % 8
    return (2 * (part % 4) + part // 4) * 16 + col


def product_place(index):
    row, col = index // 16, index % 16
    return 8 * col + 4 * (row % 2) + row // 2


def to_plane(block):
    devices = lax.axis_size("col")
    sent = jnp.broadcast_to(block[None], (devices, *block.shape))
    return lax.all_to_all(sent, "col", 0, 0, tiled=True).reshape(-1, block.shape[-1])


def halves(a):
    high = a.astype(jnp.bfloat16)
    return high, (a - high.astype(jnp.float32)).astype(jnp.bfloat16)


def near_full(a, b, dims):
    (ah, al), (bh, bl) = a, b
    dims = (dims, ((), ()))

    def one(p, q):
        return lax.dot_general(p, q, dims, preferred_element_type=jnp.float32)

    return one(ah, bh) + (one(ah, bl) + one(al, bh))


def products_kernel(core_ref, cov_ref, rows_ref, kept_ref, given_ref, t_ref):
    core = core_ref[0]
    block = t_ref.shape[0] // 8
    cut = 2 * block
    right = halves(rows_ref[...])
    for i in range(4):
        t_ref[pl.ds(i * cut, cut), :] = near_full(halves(cov_ref[pl.ds(i * cut, cut), :]), right, ((1,), (0,)))
    for ref, at in ((kept_ref, core), (given_ref, 1 - core)):
        for i in range(4):
            ref[i] = t_ref[pl.ds(pl.multiple_of((4 * at + i) * block, 8), block), :]


def inner_kernel(core_ref, kept_ref, given_ref, own_ref, other_ref, kept_out_ref, given_out_ref, m_ref):
    share = m_ref.shape[0] // 8
    first = ((0,), (0,))
    m_ref[...] = near_full(halves(own_ref[...]), halves(kept_ref[...]), first) + near_full(
        halves(other_ref[...]), halves(given_ref[...]), first
    )
    for ref, at in ((kept_out_ref, core_ref[0]), (given_out_ref, 1 - core_ref[0])):
        for i in range(4):
            ref[i] = m_ref[pl.ds(pl.multiple_of((4 * at + i) * share, 8), share), :]


SCALAR = pl.BlockSpec(memory_space=pltpu.SMEM)
VMEM = pl.BlockSpec(memory_space=pltpu.VMEM)
FAR = pl.BlockSpec(memory_space=pltpu.HBM)


def products(core, cov, rows):
    n, width = cov.shape[0], rows.shape[1]
    exchange = pltpu.VMEM((4, n // 8, width), jnp.float32)
    return pl.pallas_call(
        products_kernel,
        out_shape=(exchange, exchange),
        in_specs=[SCALAR, VMEM, VMEM],
        out_specs=(VMEM, VMEM),
        scratch_shapes=[pltpu.VMEM((n, width), jnp.float32)],
        cost_estimate=pl.CostEstimate(
            flops=6 * n * width * rows.shape[0], bytes_accessed=4 * cov.size, transcendentals=0
        ),
        compiler_params=pltpu.CompilerParams(vmem_limit_bytes=20 << 20),
    )(core.reshape(1), cov, rows)


def inner_of(core, kept, given, own, other):
    width = own.shape[1]
    exchange = pltpu.VMEM((4, width // 8, width), jnp.float32)
    tall = (own.shape[0], width)
    return pl.pallas_call(
        inner_kernel,
        out_shape=(exchange, exchange),
        in_specs=[SCALAR] + [VMEM] * 4,
        out_specs=(VMEM, VMEM),
        scratch_shapes=[pltpu.VMEM((width, width), jnp.float32)],
        cost_estimate=pl.CostEstimate(
            flops=12 * own.size * width, bytes_accessed=16 * own.size, transcendentals=0
        ),
        compiler_params=pltpu.CompilerParams(vmem_limit_bytes=10 << 20),
    )(core.reshape(1), kept.reshape(tall), given.reshape(tall), own, other)


def pieces_kernel(z_ref, kept_ref, mate_ref, *out_refs):
    for d, ref in enumerate(out_refs):
        at = z_ref[0] ^ d
        ref[...] = kept_ref[at] + mate_ref[at]


def pieces(z, kept, mate):
    return pl.pallas_call(
        pieces_kernel,
        out_shape=(pltpu.VMEM(kept.shape[1:], jnp.float32),) * 4,
        in_specs=[SCALAR, VMEM, VMEM],
        out_specs=(VMEM,) * 4,
        compiler_params=pltpu.CompilerParams(vmem_limit_bytes=4 << 20),
    )(z.reshape(1), kept, mate)


def total_kernel(a_ref, b_ref, c_ref, d_ref, out_ref):
    out_ref[...] = (a_ref[...] + b_ref[...]) + (c_ref[...] + d_ref[...])


def total_of(terms):
    return pl.pallas_call(
        total_kernel,
        out_shape=pltpu.VMEM(terms[0].shape, jnp.float32),
        in_specs=[VMEM] * 4,
        out_specs=VMEM,
        compiler_params=pltpu.CompilerParams(vmem_limit_bytes=2 << 20),
    )(*terms)


def join_kernel(product_ref, a_ref, b_ref, c_ref, d_ref, out_ref):
    block = product_ref.shape[0]
    out_ref[:block, :] = product_ref[...]
    out_ref[block:, :] = (a_ref[...] + b_ref[...]) + (c_ref[...] + d_ref[...])


def join(product, shares):
    depth = product.shape[0] + shares[0].shape[0]
    return pl.pallas_call(
        join_kernel,
        out_shape=pltpu.VMEM((depth, product.shape[1]), jnp.float32),
        in_specs=[VMEM] * 5,
        out_specs=VMEM,
        compiler_params=pltpu.CompilerParams(vmem_limit_bytes=2 << 20),
    )(product, *shares)


def pack_kernel(z_ref, *refs):
    for d, piece in enumerate(refs[:-1]):
        refs[-1][z_ref[0] ^ d] = piece[...]


def pack(z, parts):
    return pl.pallas_call(
        pack_kernel,
        out_shape=pltpu.VMEM((4, *parts[0].shape), jnp.float32),
        in_specs=[SCALAR] + [VMEM] * 4,
        out_specs=VMEM,
        compiler_params=pltpu.CompilerParams(vmem_limit_bytes=4 << 20),
    )(z.reshape(1), *parts)


def columns_kernel(far_ref, own_ref, sems):
    batch = far_ref.shape[2]
    copies = [
        pltpu.make_async_copy(far_ref.at[i], own_ref.at[:, pl.ds(i * batch, batch)], sems.at[i])
        for i in range(far_ref.shape[0])
    ]
    for copy in copies:
        copy.start()
    for copy in copies:
        copy.wait()


def columns_of(features):
    steps, block, batch = features.shape
    return pl.pallas_call(
        columns_kernel,
        out_shape=pltpu.VMEM((block, steps * batch), jnp.float32),
        in_specs=[FAR],
        out_specs=VMEM,
        scratch_shapes=[pltpu.SemaphoreType.DMA((steps,))],
        compiler_params=pltpu.CompilerParams(vmem_limit_bytes=2 << 20),
    )(pltpu.with_memory_space_constraint(features, pltpu.HBM))


def update_kernel(cov_ref, rows_ref, gain_ref, far_ref, out_ref, sems):
    cut = cov_ref.shape[0] // 2
    rows = halves(rows_ref[...])
    copies = []
    for i in range(2):
        at = pl.ds(i * cut, cut)
        out_ref[at, :] = cov_ref[at, :] - near_full(halves(gain_ref[at, :]), rows, ((1,), (1,)))
        copies.append(pltpu.make_async_copy(out_ref.at[at], far_ref.at[at], sems.at[i]))
        copies[-1].start()
    for copy in copies:
        copy.wait()


def update(cov, rows, gain):
    return pl.pallas_call(
        update_kernel,
        out_shape=pltpu.HBM(cov.shape, jnp.float32),
        in_specs=[VMEM, VMEM, VMEM],
        out_specs=FAR,
        scratch_shapes=[pltpu.VMEM(cov.shape, jnp.float32), pltpu.SemaphoreType.DMA((2,))],
        cost_estimate=pl.CostEstimate(
            flops=6 * cov.size * rows.shape[1], bytes_accessed=4 * cov.size, transcendentals=0
        ),
        compiler_params=pltpu.CompilerParams(vmem_limit_bytes=20 << 20),
    )(cov, pltpu.with_memory_space_constraint(rows, pltpu.VMEM), gain)


def gain_kernel(core_ref, own_ref, other_ref, inv_ref, out_ref):
    block = out_ref.shape[0] // 8
    inverse = halves(inv_ref[...])
    for ref, at in ((own_ref, core_ref[0]), (other_ref, 1 - core_ref[0])):
        for j in range(4):
            out_ref[pl.ds(pl.multiple_of((4 * at + j) * block, 8), block), :] = ref[j, :block, :]
    out_ref[...] = near_full(halves(out_ref[...]), inverse, ((1,), (0,)))


def gain_of(core, own, other, inverse, block):
    return pl.pallas_call(
        gain_kernel,
        out_shape=pltpu.VMEM((8 * block, own.shape[2]), jnp.float32),
        in_specs=[SCALAR, VMEM, VMEM, VMEM],
        out_specs=VMEM,
        compiler_params=pltpu.CompilerParams(vmem_limit_bytes=6 << 20),
    )(core.reshape(1), own, other, inverse)


def hold_kernel(far_ref, near_ref, sems):
    cut = near_ref.shape[0] // 4
    copies = [
        pltpu.make_async_copy(far_ref.at[pl.ds(i * cut, cut)], near_ref.at[pl.ds(i * cut, cut)], sems.at[i])
        for i in range(4)
    ]
    for copy in copies:
        copy.start()
    for copy in copies:
        copy.wait()


def hold(cov):
    cov = pltpu.with_memory_space_constraint(cov, pltpu.HBM)
    return pl.pallas_call(
        hold_kernel,
        out_shape=pltpu.VMEM(cov.shape, jnp.float32),
        in_specs=[pl.BlockSpec(memory_space=pltpu.HBM)],
        out_specs=VMEM,
        scratch_shapes=[pltpu.SemaphoreType.DMA((4,))],
        compiler_params=pltpu.CompilerParams(vmem_limit_bytes=4 << 20),
    )(cov)


def invert_kernel(core_ref, own_ref, other_ref, noise_ref, out_ref, m_ref):
    n = m_ref.shape[0]
    share = n // 8
    for ref, at in ((own_ref, core_ref[0]), (other_ref, 1 - core_ref[0])):
        for j in range(4):
            m_ref[pl.ds(pl.multiple_of((4 * at + j) * share, 8), share), :] = ref[j, ref.shape[1] - share :, :]
    eye = lax.broadcasted_iota(jnp.int32, (n, n), 0) == lax.broadcasted_iota(jnp.int32, (n, n), 1)
    one = jnp.where(eye, 1.0, 0.0).astype(jnp.float32)
    system = m_ref[...] + jnp.where(eye, noise_ref[...], 0.0)
    diag = jnp.where(eye, system, 0.0)
    across = lax.rsqrt(jnp.sum(diag, axis=0, keepdims=True))
    down = lax.rsqrt(jnp.sum(diag, axis=1, keepdims=True))
    scaled = system * down * across
    bound = jnp.max(jnp.sum(jnp.abs(scaled), axis=1, keepdims=True), axis=0, keepdims=True)
    alpha = 2.0 / (1.0 + bound)
    err = one - alpha * scaled
    start = alpha * (one + err)

    def fast(a, b):
        return jnp.dot(a.astype(jnp.bfloat16), b.astype(jnp.bfloat16), preferred_element_type=jnp.float32)

    def full(a, b):
        return jnp.dot(a, b, precision=HIGHEST, preferred_element_type=jnp.float32)

    err2 = fast(err, err)
    err4 = fast(err2, err2)
    guess = start + fast(start, err2)
    guess = guess + fast(guess, err4)

    def norm(r):
        return jnp.max(jnp.sum(jnp.abs(r), axis=0, keepdims=True))

    rest = one - full(scaled, guess)
    size = norm(rest)

    def go_on(state):
        return jnp.logical_and(state[2] >= 1e-3, state[3] < 60)

    def finished(multiply, y, r, bound):
        def refine(state):
            y, r, _, count = state
            y = y + multiply(y, r)
            r = one - full(scaled, y)
            return y, r, norm(r), count + 1

        y, r, _, _ = lax.while_loop(go_on, refine, (y, r, bound, jnp.int32(0)))
        return y + multiply(y, r)

    guess = lax.cond(
        size < 0.5,
        lambda: finished(fast, guess, rest, size),
        lambda: finished(full, start, one - full(scaled, start), jnp.float32(1.0)),
    )
    out_ref[...] = guess * down * across


def inverse_of(core, own, other, noise):
    n = noise.shape[1]
    return pl.pallas_call(
        invert_kernel,
        out_shape=pltpu.VMEM((n, n), jnp.float32),
        in_specs=[SCALAR, VMEM, VMEM, VMEM],
        out_specs=VMEM,
        scratch_shapes=[pltpu.VMEM((n, n), jnp.float32)],
        cost_estimate=pl.CostEstimate(flops=2 * n**3 * 40, bytes_accessed=4 * n * n * 3, transcendentals=n),
        compiler_params=pltpu.CompilerParams(vmem_limit_bytes=12 << 20),
    )(core.reshape(1), own, other, noise)


def step(covariance, features, noise):
    r = lax.axis_index("row")
    z, core = r >> 1, r & 1
    steps, block, batch = features.shape
    width = steps * batch
    own = columns_of(features)
    turned = hold(covariance.T)

    row_features = to_plane(own)
    apart = to_place(own, feature_place)
    za = side(apart, to_xor(apart, "row", 2), z & 1)
    zb = side(za, to_xor(za, "row", 6), z >> 1)
    quad = zb.reshape(4 * block, width)

    kept, given = products(core, turned, row_features)
    terms = pieces(z, kept, to_xor(given, "row", 1))
    kept_inner, given_inner = inner_of(core, kept, given, quad, to_xor(quad, "row", 1))
    shares = pieces(z, kept_inner, to_xor(given_inner, "row", 1))
    share = total_of([shares[0]] + [to_xor(shares[d], "row", 2 * d) for d in (1, 2, 3)])
    product = total_of([terms[0]] + [to_xor(terms[d], "row", 2 * d) for d in (1, 2, 3)])

    share = total_of([share] + [to_xor(share, "col", d) for d in (1, 2, 3)])
    joined = join(product, [share] + [to_xor(share, "col", 4 * d) for d in (1, 2, 3)])
    packed = pack(z, [joined] + [to_xor(joined, "row", 2 * d) for d in (1, 2, 3)])
    mate = to_xor(packed, "row", 1)

    product_rows = to_plane(to_place(product, product_place))

    inverse = inverse_of(core, packed, mate, noise.reshape(1, width))
    gain = gain_of(core, packed, mate, inverse, block)
    return update(turned, product_rows, gain).T


def solution(mesh):
    specs = (P("row", "col"), P(None, ("row", "col"), None), P())
    return jax.shard_map(step, mesh=mesh, in_specs=specs, out_specs=P("row", "col"), check_vma=False)
```

```python
import jax
import jax.numpy as jnp
from jax import lax
from jax.experimental import pallas as pl
from jax.experimental.pallas import tpu as pltpu
from jax.sharding import PartitionSpec as P


HIGHEST = lax.Precision.HIGHEST


def to_xor(value, axis, bits):
    size = lax.axis_size(axis)
    return lax.ppermute(value, axis, [(i, i ^ bits) for i in range(size)])


def to_place(value, owner):
    return lax.ppermute(value, ("row", "col"), [(i, owner(i)) for i in range(128)])


def side(a, b, bit):
    first = jnp.where(bit == 0, a, b)
    second = jnp.where(bit == 0, b, a)
    return jnp.stack([first, second])


def feature_place(index):
    col, part = index // 8, index % 8
    return (2 * (part % 4) + part // 4) * 16 + col


def product_place(index):
    row, col = index // 16, index % 16
    return 8 * col + 4 * (row % 2) + row // 2


def to_plane(block):
    devices = lax.axis_size("col")
    sent = jnp.broadcast_to(block[None], (devices, *block.shape))
    return lax.all_to_all(sent, "col", 0, 0, tiled=True).reshape(-1, block.shape[-1])


def halves(a):
    high = a.astype(jnp.bfloat16)
    return high, (a - high.astype(jnp.float32)).astype(jnp.bfloat16)


def near_full(a, b, dims):
    (ah, al), (bh, bl) = a, b
    dims = (dims, ((), ()))

    def one(p, q):
        return lax.dot_general(p, q, dims, preferred_element_type=jnp.float32)

    return one(ah, bh) + (one(ah, bl) + one(al, bh))


def products_kernel(core_ref, cov_ref, rows_ref, kept_ref, given_ref, t_ref):
    core = core_ref[0]
    block = t_ref.shape[0] // 8
    cut = 2 * block
    right = halves(rows_ref[...])
    for i in range(4):
        t_ref[pl.ds(i * cut, cut), :] = near_full(halves(cov_ref[pl.ds(i * cut, cut), :]), right, ((1,), (0,)))
    for ref, at in ((kept_ref, core), (given_ref, 1 - core)):
        for i in range(4):
            ref[i] = t_ref[pl.ds(pl.multiple_of((4 * at + i) * block, 8), block), :]


def inner_kernel(core_ref, kept_ref, given_ref, own_ref, other_ref, kept_out_ref, given_out_ref, m_ref):
    share = m_ref.shape[0] // 8
    first = ((0,), (0,))
    m_ref[...] = near_full(halves(own_ref[...]), halves(kept_ref[...]), first) + near_full(
        halves(other_ref[...]), halves(given_ref[...]), first
    )
    for ref, at in ((kept_out_ref, core_ref[0]), (given_out_ref, 1 - core_ref[0])):
        for i in range(4):
            ref[i] = m_ref[pl.ds(pl.multiple_of((4 * at + i) * share, 8), share), :]


SCALAR = pl.BlockSpec(memory_space=pltpu.SMEM)
VMEM = pl.BlockSpec(memory_space=pltpu.VMEM)
FAR = pl.BlockSpec(memory_space=pltpu.HBM)


def products(core, cov, rows):
    n, width = cov.shape[0], rows.shape[1]
    exchange = pltpu.VMEM((4, n // 8, width), jnp.float32)
    return pl.pallas_call(
        products_kernel,
        out_shape=(exchange, exchange),
        in_specs=[SCALAR, VMEM, VMEM],
        out_specs=(VMEM, VMEM),
        scratch_shapes=[pltpu.VMEM((n, width), jnp.float32)],
        cost_estimate=pl.CostEstimate(
            flops=6 * n * width * rows.shape[0], bytes_accessed=4 * cov.size, transcendentals=0
        ),
        compiler_params=pltpu.CompilerParams(vmem_limit_bytes=20 << 20),
    )(core.reshape(1), cov, rows)


def inner_of(core, kept, given, own, other):
    width = own.shape[1]
    exchange = pltpu.VMEM((4, width // 8, width), jnp.float32)
    tall = (own.shape[0], width)
    return pl.pallas_call(
        inner_kernel,
        out_shape=(exchange, exchange),
        in_specs=[SCALAR] + [VMEM] * 4,
        out_specs=(VMEM, VMEM),
        scratch_shapes=[pltpu.VMEM((width, width), jnp.float32)],
        cost_estimate=pl.CostEstimate(
            flops=12 * own.size * width, bytes_accessed=16 * own.size, transcendentals=0
        ),
        compiler_params=pltpu.CompilerParams(vmem_limit_bytes=10 << 20),
    )(core.reshape(1), kept.reshape(tall), given.reshape(tall), own, other)


def pieces_kernel(z_ref, kept_ref, mate_ref, *out_refs):
    for d, ref in enumerate(out_refs):
        at = z_ref[0] ^ d
        ref[...] = kept_ref[at] + mate_ref[at]


def pieces(z, kept, mate):
    return pl.pallas_call(
        pieces_kernel,
        out_shape=(pltpu.VMEM(kept.shape[1:], jnp.float32),) * 4,
        in_specs=[SCALAR, VMEM, VMEM],
        out_specs=(VMEM,) * 4,
        compiler_params=pltpu.CompilerParams(vmem_limit_bytes=4 << 20),
    )(z.reshape(1), kept, mate)


def total_kernel(a_ref, b_ref, c_ref, d_ref, out_ref):
    out_ref[...] = (a_ref[...] + b_ref[...]) + (c_ref[...] + d_ref[...])


def total_of(terms):
    return pl.pallas_call(
        total_kernel,
        out_shape=pltpu.VMEM(terms[0].shape, jnp.float32),
        in_specs=[VMEM] * 4,
        out_specs=VMEM,
        compiler_params=pltpu.CompilerParams(vmem_limit_bytes=2 << 20),
    )(*terms)


def join_kernel(product_ref, a_ref, b_ref, c_ref, d_ref, out_ref):
    block = product_ref.shape[0]
    out_ref[:block, :] = product_ref[...]
    out_ref[block:, :] = (a_ref[...] + b_ref[...]) + (c_ref[...] + d_ref[...])


def join(product, shares):
    depth = product.shape[0] + shares[0].shape[0]
    return pl.pallas_call(
        join_kernel,
        out_shape=pltpu.VMEM((depth, product.shape[1]), jnp.float32),
        in_specs=[VMEM] * 5,
        out_specs=VMEM,
        compiler_params=pltpu.CompilerParams(vmem_limit_bytes=2 << 20),
    )(product, *shares)


def pack_kernel(z_ref, *refs):
    for d, piece in enumerate(refs[:-1]):
        refs[-1][z_ref[0] ^ d] = piece[...]


def pack(z, parts):
    return pl.pallas_call(
        pack_kernel,
        out_shape=pltpu.VMEM((4, *parts[0].shape), jnp.float32),
        in_specs=[SCALAR] + [VMEM] * 4,
        out_specs=VMEM,
        compiler_params=pltpu.CompilerParams(vmem_limit_bytes=4 << 20),
    )(z.reshape(1), *parts)


def columns_kernel(far_ref, own_ref, sems):
    batch = far_ref.shape[2]
    copies = [
        pltpu.make_async_copy(far_ref.at[i], own_ref.at[:, pl.ds(i * batch, batch)], sems.at[i])
        for i in range(far_ref.shape[0])
    ]
    for copy in copies:
        copy.start()
    for copy in copies:
        copy.wait()


def columns_of(features):
    steps, block, batch = features.shape
    return pl.pallas_call(
        columns_kernel,
        out_shape=pltpu.VMEM((block, steps * batch), jnp.float32),
        in_specs=[FAR],
        out_specs=VMEM,
        scratch_shapes=[pltpu.SemaphoreType.DMA((steps,))],
        compiler_params=pltpu.CompilerParams(vmem_limit_bytes=2 << 20),
    )(pltpu.with_memory_space_constraint(features, pltpu.HBM))


def update_kernel(cov_ref, rows_ref, gain_ref, far_ref, out_ref, sems):
    cut = cov_ref.shape[0] // 2
    rows = halves(rows_ref[...])
    copies = []
    for i in range(2):
        at = pl.ds(i * cut, cut)
        out_ref[at, :] = cov_ref[at, :] - near_full(halves(gain_ref[at, :]), rows, ((1,), (1,)))
        copies.append(pltpu.make_async_copy(out_ref.at[at], far_ref.at[at], sems.at[i]))
        copies[-1].start()
    for copy in copies:
        copy.wait()


def update(cov, rows, gain):
    return pl.pallas_call(
        update_kernel,
        out_shape=pltpu.HBM(cov.shape, jnp.float32),
        in_specs=[VMEM, VMEM, VMEM],
        out_specs=FAR,
        scratch_shapes=[pltpu.VMEM(cov.shape, jnp.float32), pltpu.SemaphoreType.DMA((2,))],
        cost_estimate=pl.CostEstimate(
            flops=6 * cov.size * rows.shape[1], bytes_accessed=4 * cov.size, transcendentals=0
        ),
        compiler_params=pltpu.CompilerParams(vmem_limit_bytes=20 << 20),
    )(cov, pltpu.with_memory_space_constraint(rows, pltpu.VMEM), gain)


def gain_kernel(core_ref, own_ref, other_ref, inv_ref, out_ref):
    block = out_ref.shape[0] // 8
    inverse = halves(inv_ref[...])
    for ref, at in ((own_ref, core_ref[0]), (other_ref, 1 - core_ref[0])):
        for j in range(4):
            out_ref[pl.ds(pl.multiple_of((4 * at + j) * block, 8), block), :] = ref[j, :block, :]
    out_ref[...] = near_full(halves(out_ref[...]), inverse, ((1,), (0,)))


def gain_of(core, own, other, inverse, block):
    return pl.pallas_call(
        gain_kernel,
        out_shape=pltpu.VMEM((8 * block, own.shape[2]), jnp.float32),
        in_specs=[SCALAR, VMEM, VMEM, VMEM],
        out_specs=VMEM,
        compiler_params=pltpu.CompilerParams(vmem_limit_bytes=6 << 20),
    )(core.reshape(1), own, other, inverse)


def hold_kernel(far_ref, near_ref, sems):
    cut = near_ref.shape[0] // 4
    copies = [
        pltpu.make_async_copy(far_ref.at[pl.ds(i * cut, cut)], near_ref.at[pl.ds(i * cut, cut)], sems.at[i])
        for i in range(4)
    ]
    for copy in copies:
        copy.start()
    for copy in copies:
        copy.wait()


def hold(cov):
    cov = pltpu.with_memory_space_constraint(cov, pltpu.HBM)
    return pl.pallas_call(
        hold_kernel,
        out_shape=pltpu.VMEM(cov.shape, jnp.float32),
        in_specs=[pl.BlockSpec(memory_space=pltpu.HBM)],
        out_specs=VMEM,
        scratch_shapes=[pltpu.SemaphoreType.DMA((4,))],
        compiler_params=pltpu.CompilerParams(vmem_limit_bytes=4 << 20),
    )(cov)


def invert_kernel(core_ref, own_ref, other_ref, noise_ref, out_ref, m_ref):
    n = m_ref.shape[0]
    share = n // 8
    for ref, at in ((own_ref, core_ref[0]), (other_ref, 1 - core_ref[0])):
        for j in range(4):
            m_ref[pl.ds(pl.multiple_of((4 * at + j) * share, 8), share), :] = ref[j, ref.shape[1] - share :, :]
    eye = lax.broadcasted_iota(jnp.int32, (n, n), 0) == lax.broadcasted_iota(jnp.int32, (n, n), 1)
    one = jnp.where(eye, 1.0, 0.0).astype(jnp.float32)
    system = m_ref[...] + jnp.where(eye, noise_ref[...], 0.0)
    diag = jnp.where(eye, system, 0.0)
    across = lax.rsqrt(jnp.sum(diag, axis=0, keepdims=True))
    down = lax.rsqrt(jnp.sum(diag, axis=1, keepdims=True))
    scaled = system * down * across
    bound = jnp.max(jnp.sum(jnp.abs(scaled), axis=1, keepdims=True), axis=0, keepdims=True)
    alpha = 2.0 / (1.0 + bound)
    err = one - alpha * scaled
    start = alpha * (one + err)

    def fast(a, b):
        return jnp.dot(a.astype(jnp.bfloat16), b.astype(jnp.bfloat16), preferred_element_type=jnp.float32)

    def full(a, b):
        return jnp.dot(a, b, precision=HIGHEST, preferred_element_type=jnp.float32)

    err2 = fast(err, err)
    err4 = fast(err2, err2)
    guess = start + fast(start, err2)
    guess = guess + fast(guess, err4)

    def norm(r):
        return jnp.max(jnp.sum(jnp.abs(r), axis=0, keepdims=True))

    rest = one - full(scaled, guess)
    size = norm(rest)

    def go_on(state):
        return jnp.logical_and(state[2] >= 1e-3, state[3] < 60)

    def finished(multiply, y, r, bound):
        def refine(state):
            y, r, _, count = state
            y = y + multiply(y, r)
            r = one - full(scaled, y)
            return y, r, norm(r), count + 1

        y, r, _, _ = lax.while_loop(go_on, refine, (y, r, bound, jnp.int32(0)))
        return y + multiply(y, r)

    def quartic():
        square = fast(rest, rest)
        better = guess + near_full(halves(guess), halves(rest), ((1,), (0,)))
        return better + fast(better, square)

    guess = lax.cond(
        size < 0.5,
        lambda: lax.cond(size < 0.05, quartic, lambda: finished(fast, guess, rest, size)),
        lambda: finished(full, start, one - full(scaled, start), jnp.float32(1.0)),
    )
    out_ref[...] = guess * down * across


def inverse_of(core, own, other, noise):
    n = noise.shape[1]
    return pl.pallas_call(
        invert_kernel,
        out_shape=pltpu.VMEM((n, n), jnp.float32),
        in_specs=[SCALAR, VMEM, VMEM, VMEM],
        out_specs=VMEM,
        scratch_shapes=[pltpu.VMEM((n, n), jnp.float32)],
        cost_estimate=pl.CostEstimate(flops=2 * n**3 * 40, bytes_accessed=4 * n * n * 3, transcendentals=n),
        compiler_params=pltpu.CompilerParams(vmem_limit_bytes=12 << 20),
    )(core.reshape(1), own, other, noise)


def step(covariance, features, noise):
    r = lax.axis_index("row")
    z, core = r >> 1, r & 1
    steps, block, batch = features.shape
    width = steps * batch
    own = columns_of(features)
    turned = hold(covariance.T)

    row_features = to_plane(own)
    apart = to_place(own, feature_place)
    za = side(apart, to_xor(apart, "row", 2), z & 1)
    zb = side(za, to_xor(za, "row", 6), z >> 1)
    quad = zb.reshape(4 * block, width)

    kept, given = products(core, turned, row_features)
    terms = pieces(z, kept, to_xor(given, "row", 1))
    kept_inner, given_inner = inner_of(core, kept, given, quad, to_xor(quad, "row", 1))
    shares = pieces(z, kept_inner, to_xor(given_inner, "row", 1))
    share = total_of([shares[0]] + [to_xor(shares[d], "row", 2 * d) for d in (1, 2, 3)])
    product = total_of([terms[0]] + [to_xor(terms[d], "row", 2 * d) for d in (1, 2, 3)])

    share = total_of([share] + [to_xor(share, "col", d) for d in (1, 2, 3)])
    joined = join(product, [share] + [to_xor(share, "col", 4 * d) for d in (1, 2, 3)])
    packed = pack(z, [joined] + [to_xor(joined, "row", 2 * d) for d in (1, 2, 3)])
    mate = to_xor(packed, "row", 1)

    product_rows = to_plane(to_place(product, product_place))

    inverse = inverse_of(core, packed, mate, noise.reshape(1, width))
    gain = gain_of(core, packed, mate, inverse, block)
    return update(turned, product_rows, gain).T


def solution(mesh):
    specs = (P("row", "col"), P(None, ("row", "col"), None), P())
    return jax.shard_map(step, mesh=mesh, in_specs=specs, out_specs=P("row", "col"), check_vma=False)
```

```python
import jax
import jax.numpy as jnp
from jax import lax
from jax.experimental import pallas as pl
from jax.experimental.pallas import tpu as pltpu
from jax.sharding import PartitionSpec as P


HIGHEST = lax.Precision.HIGHEST


def to_xor(value, axis, bits):
    size = lax.axis_size(axis)
    return lax.ppermute(value, axis, [(i, i ^ bits) for i in range(size)])


def to_place(value, owner):
    return lax.ppermute(value, ("row", "col"), [(i, owner(i)) for i in range(128)])


def side(a, b, bit):
    first = jnp.where(bit == 0, a, b)
    second = jnp.where(bit == 0, b, a)
    return jnp.stack([first, second])


def feature_place(index):
    col, part = index // 8, index % 8
    return (2 * (part % 4) + part // 4) * 16 + col


def product_place(index):
    row, col = index // 16, index % 16
    return 8 * col + 4 * (row % 2) + row // 2


def to_plane(block):
    devices = lax.axis_size("col")
    sent = jnp.broadcast_to(block[None], (devices, *block.shape))
    return lax.all_to_all(sent, "col", 0, 0, tiled=True).reshape(-1, block.shape[-1])


def halves(a):
    high = a.astype(jnp.bfloat16)
    return high, (a - high.astype(jnp.float32)).astype(jnp.bfloat16)


def near_full(a, b, dims):
    (ah, al), (bh, bl) = a, b
    dims = (dims, ((), ()))

    def one(p, q):
        return lax.dot_general(p, q, dims, preferred_element_type=jnp.float32)

    return one(ah, bh) + (one(ah, bl) + one(al, bh))


def products_kernel(core_ref, cov_ref, rows_ref, kept_ref, given_ref, t_ref):
    core = core_ref[0]
    block = t_ref.shape[0] // 8
    cut = 2 * block
    right = halves(rows_ref[...])
    for i in range(4):
        t_ref[pl.ds(i * cut, cut), :] = near_full(halves(cov_ref[pl.ds(i * cut, cut), :]), right, ((1,), (0,)))
    for ref, at in ((kept_ref, core), (given_ref, 1 - core)):
        for i in range(4):
            ref[i] = t_ref[pl.ds(pl.multiple_of((4 * at + i) * block, 8), block), :]


def inner_kernel(core_ref, kept_ref, given_ref, own_ref, other_ref, kept_out_ref, given_out_ref, m_ref):
    share = m_ref.shape[0] // 8
    first = ((0,), (0,))
    m_ref[...] = near_full(halves(own_ref[...]), halves(kept_ref[...]), first) + near_full(
        halves(other_ref[...]), halves(given_ref[...]), first
    )
    for ref, at in ((kept_out_ref, core_ref[0]), (given_out_ref, 1 - core_ref[0])):
        for i in range(4):
            ref[i] = m_ref[pl.ds(pl.multiple_of((4 * at + i) * share, 8), share), :]


SCALAR = pl.BlockSpec(memory_space=pltpu.SMEM)
VMEM = pl.BlockSpec(memory_space=pltpu.VMEM)
FAR = pl.BlockSpec(memory_space=pltpu.HBM)


def products(core, cov, rows):
    n, width = cov.shape[0], rows.shape[1]
    exchange = pltpu.VMEM((4, n // 8, width), jnp.float32)
    return pl.pallas_call(
        products_kernel,
        out_shape=(exchange, exchange),
        in_specs=[SCALAR, VMEM, VMEM],
        out_specs=(VMEM, VMEM),
        scratch_shapes=[pltpu.VMEM((n, width), jnp.float32)],
        cost_estimate=pl.CostEstimate(
            flops=6 * n * width * rows.shape[0], bytes_accessed=4 * cov.size, transcendentals=0
        ),
        compiler_params=pltpu.CompilerParams(vmem_limit_bytes=20 << 20),
    )(core.reshape(1), cov, rows)


def inner_of(core, kept, given, own, other):
    width = own.shape[1]
    exchange = pltpu.VMEM((4, width // 8, width), jnp.float32)
    tall = (own.shape[0], width)
    return pl.pallas_call(
        inner_kernel,
        out_shape=(exchange, exchange),
        in_specs=[SCALAR] + [VMEM] * 4,
        out_specs=(VMEM, VMEM),
        scratch_shapes=[pltpu.VMEM((width, width), jnp.float32)],
        cost_estimate=pl.CostEstimate(
            flops=12 * own.size * width, bytes_accessed=16 * own.size, transcendentals=0
        ),
        compiler_params=pltpu.CompilerParams(vmem_limit_bytes=10 << 20),
    )(core.reshape(1), kept.reshape(tall), given.reshape(tall), own, other)


def pieces_kernel(z_ref, kept_ref, mate_ref, *out_refs):
    for d, ref in enumerate(out_refs):
        at = z_ref[0] ^ d
        ref[...] = kept_ref[at] + mate_ref[at]


def pieces(z, kept, mate):
    return pl.pallas_call(
        pieces_kernel,
        out_shape=(pltpu.VMEM(kept.shape[1:], jnp.float32),) * 4,
        in_specs=[SCALAR, VMEM, VMEM],
        out_specs=(VMEM,) * 4,
        compiler_params=pltpu.CompilerParams(vmem_limit_bytes=4 << 20),
    )(z.reshape(1), kept, mate)


def total_kernel(a_ref, b_ref, c_ref, d_ref, out_ref):
    out_ref[...] = (a_ref[...] + b_ref[...]) + (c_ref[...] + d_ref[...])


def total_of(terms):
    return pl.pallas_call(
        total_kernel,
        out_shape=pltpu.VMEM(terms[0].shape, jnp.float32),
        in_specs=[VMEM] * 4,
        out_specs=VMEM,
        compiler_params=pltpu.CompilerParams(vmem_limit_bytes=2 << 20),
    )(*terms)


def join_kernel(product_ref, a_ref, b_ref, c_ref, d_ref, out_ref):
    block = product_ref.shape[0]
    out_ref[:block, :] = product_ref[...]
    out_ref[block:, :] = (a_ref[...] + b_ref[...]) + (c_ref[...] + d_ref[...])


def join(product, shares):
    depth = product.shape[0] + shares[0].shape[0]
    return pl.pallas_call(
        join_kernel,
        out_shape=pltpu.VMEM((depth, product.shape[1]), jnp.float32),
        in_specs=[VMEM] * 5,
        out_specs=VMEM,
        compiler_params=pltpu.CompilerParams(vmem_limit_bytes=2 << 20),
    )(product, *shares)


def pack_kernel(z_ref, *refs):
    for d, piece in enumerate(refs[:-1]):
        refs[-1][z_ref[0] ^ d] = piece[...]


def pack(z, parts):
    return pl.pallas_call(
        pack_kernel,
        out_shape=pltpu.VMEM((4, *parts[0].shape), jnp.float32),
        in_specs=[SCALAR] + [VMEM] * 4,
        out_specs=VMEM,
        compiler_params=pltpu.CompilerParams(vmem_limit_bytes=4 << 20),
    )(z.reshape(1), *parts)


def columns_kernel(far_ref, own_ref, sems):
    batch = far_ref.shape[2]
    copies = [
        pltpu.make_async_copy(far_ref.at[i], own_ref.at[:, pl.ds(i * batch, batch)], sems.at[i])
        for i in range(far_ref.shape[0])
    ]
    for copy in copies:
        copy.start()
    for copy in copies:
        copy.wait()


def columns_of(features):
    steps, block, batch = features.shape
    return pl.pallas_call(
        columns_kernel,
        out_shape=pltpu.VMEM((block, steps * batch), jnp.float32),
        in_specs=[FAR],
        out_specs=VMEM,
        scratch_shapes=[pltpu.SemaphoreType.DMA((steps,))],
        compiler_params=pltpu.CompilerParams(vmem_limit_bytes=2 << 20),
    )(pltpu.with_memory_space_constraint(features, pltpu.HBM))


def update_kernel(cov_ref, rows_ref, gain_ref, far_ref, out_ref, sems):
    cut = cov_ref.shape[0] // 2
    rows = halves(rows_ref[...])
    copies = []
    for i in range(2):
        at = pl.ds(i * cut, cut)
        out_ref[at, :] = cov_ref[at, :] - near_full(halves(gain_ref[at, :]), rows, ((1,), (1,)))
        copies.append(pltpu.make_async_copy(out_ref.at[at], far_ref.at[at], sems.at[i]))
        copies[-1].start()
    for copy in copies:
        copy.wait()


def update(cov, rows, gain):
    return pl.pallas_call(
        update_kernel,
        out_shape=pltpu.HBM(cov.shape, jnp.float32),
        in_specs=[VMEM, VMEM, VMEM],
        out_specs=FAR,
        scratch_shapes=[pltpu.VMEM(cov.shape, jnp.float32), pltpu.SemaphoreType.DMA((2,))],
        cost_estimate=pl.CostEstimate(
            flops=6 * cov.size * rows.shape[1], bytes_accessed=4 * cov.size, transcendentals=0
        ),
        compiler_params=pltpu.CompilerParams(vmem_limit_bytes=20 << 20),
    )(cov, pltpu.with_memory_space_constraint(rows, pltpu.VMEM), gain)


def hold_kernel(far_ref, near_ref, sems):
    cut = near_ref.shape[0] // 4
    copies = [
        pltpu.make_async_copy(far_ref.at[pl.ds(i * cut, cut)], near_ref.at[pl.ds(i * cut, cut)], sems.at[i])
        for i in range(4)
    ]
    for copy in copies:
        copy.start()
    for copy in copies:
        copy.wait()


def hold(cov):
    cov = pltpu.with_memory_space_constraint(cov, pltpu.HBM)
    return pl.pallas_call(
        hold_kernel,
        out_shape=pltpu.VMEM(cov.shape, jnp.float32),
        in_specs=[pl.BlockSpec(memory_space=pltpu.HBM)],
        out_specs=VMEM,
        scratch_shapes=[pltpu.SemaphoreType.DMA((4,))],
        compiler_params=pltpu.CompilerParams(vmem_limit_bytes=4 << 20),
    )(cov)


def invert_kernel(core_ref, own_ref, other_ref, noise_ref, out_ref, m_ref):
    n = m_ref.shape[0]
    share = n // 8
    for ref, at in ((own_ref, core_ref[0]), (other_ref, 1 - core_ref[0])):
        for j in range(4):
            m_ref[pl.ds(pl.multiple_of((4 * at + j) * share, 8), share), :] = ref[j, ref.shape[1] - share :, :]
    eye = lax.broadcasted_iota(jnp.int32, (n, n), 0) == lax.broadcasted_iota(jnp.int32, (n, n), 1)
    one = jnp.where(eye, 1.0, 0.0).astype(jnp.float32)
    system = m_ref[...] + jnp.where(eye, noise_ref[...], 0.0)
    diag = jnp.where(eye, system, 0.0)
    across = lax.rsqrt(jnp.sum(diag, axis=0, keepdims=True))
    down = lax.rsqrt(jnp.sum(diag, axis=1, keepdims=True))
    scaled = system * down * across
    bound = jnp.max(jnp.sum(jnp.abs(scaled), axis=1, keepdims=True), axis=0, keepdims=True)
    alpha = 2.0 / (1.0 + bound)
    err = one - alpha * scaled
    start = alpha * (one + err)

    def fast(a, b):
        return jnp.dot(a.astype(jnp.bfloat16), b.astype(jnp.bfloat16), preferred_element_type=jnp.float32)

    def full(a, b):
        return jnp.dot(a, b, precision=HIGHEST, preferred_element_type=jnp.float32)

    err2 = fast(err, err)
    err4 = fast(err2, err2)
    guess = start + fast(start, err2)
    guess = guess + fast(guess, err4)

    def norm(r):
        return jnp.max(jnp.sum(jnp.abs(r), axis=0, keepdims=True))

    rest = one - full(scaled, guess)
    size = norm(rest)

    def go_on(state):
        return jnp.logical_and(state[2] >= 1e-3, state[3] < 60)

    def finished(multiply, y, r, bound):
        def refine(state):
            y, r, _, count = state
            y = y + multiply(y, r)
            r = one - full(scaled, y)
            return y, r, norm(r), count + 1

        y, r, _, _ = lax.while_loop(go_on, refine, (y, r, bound, jnp.int32(0)))
        return y + multiply(y, r)

    def quartic():
        square = fast(rest, rest)
        better = guess + near_full(halves(guess), halves(rest), ((1,), (0,)))
        return better + fast(better, square)

    guess = lax.cond(
        size < 0.5,
        lambda: lax.cond(size < 0.05, quartic, lambda: finished(fast, guess, rest, size)),
        lambda: finished(full, start, one - full(scaled, start), jnp.float32(1.0)),
    )
    inverse = halves(guess * down * across)
    block = out_ref.shape[0] // 8
    for ref, at in ((own_ref, core_ref[0]), (other_ref, 1 - core_ref[0])):
        for j in range(4):
            out_ref[pl.ds(pl.multiple_of((4 * at + j) * block, 8), block), :] = ref[j, :block, :]
    out_ref[...] = near_full(halves(out_ref[...]), inverse, ((1,), (0,)))


def gain_of(core, own, other, noise, block):
    n = noise.shape[1]
    return pl.pallas_call(
        invert_kernel,
        out_shape=pltpu.VMEM((8 * block, n), jnp.float32),
        in_specs=[SCALAR, VMEM, VMEM, VMEM],
        out_specs=VMEM,
        scratch_shapes=[pltpu.VMEM((n, n), jnp.float32)],
        cost_estimate=pl.CostEstimate(flops=2 * n**3 * 40, bytes_accessed=4 * n * n * 3, transcendentals=n),
        compiler_params=pltpu.CompilerParams(vmem_limit_bytes=12 << 20),
    )(core.reshape(1), own, other, noise)


def step(covariance, features, noise):
    r = lax.axis_index("row")
    z, core = r >> 1, r & 1
    steps, block, batch = features.shape
    width = steps * batch
    own = columns_of(features)
    turned = hold(covariance.T)

    row_features = to_plane(own)
    apart = to_place(own, feature_place)
    za = side(apart, to_xor(apart, "row", 2), z & 1)
    zb = side(za, to_xor(za, "row", 6), z >> 1)
    quad = zb.reshape(4 * block, width)

    kept, given = products(core, turned, row_features)
    terms = pieces(z, kept, to_xor(given, "row", 1))
    kept_inner, given_inner = inner_of(core, kept, given, quad, to_xor(quad, "row", 1))
    shares = pieces(z, kept_inner, to_xor(given_inner, "row", 1))
    share = total_of([shares[0]] + [to_xor(shares[d], "row", 2 * d) for d in (1, 2, 3)])
    product = total_of([terms[0]] + [to_xor(terms[d], "row", 2 * d) for d in (1, 2, 3)])

    share = total_of([share] + [to_xor(share, "col", d) for d in (1, 2, 3)])
    joined = join(product, [share] + [to_xor(share, "col", 4 * d) for d in (1, 2, 3)])
    packed = pack(z, [joined] + [to_xor(joined, "row", 2 * d) for d in (1, 2, 3)])
    mate = to_xor(packed, "row", 1)

    product_rows = to_plane(to_place(product, product_place))

    gain = gain_of(core, packed, mate, noise.reshape(1, width), block)
    return update(turned, product_rows, gain).T


def solution(mesh):
    specs = (P("row", "col"), P(None, ("row", "col"), None), P())
    return jax.shard_map(step, mesh=mesh, in_specs=specs, out_specs=P("row", "col"), check_vma=False)
```
